512 devices in a mesh: freq: 32 (over x, z_lo), chan: 16 (over y, z_hi, core).
Axes of the slice: x: 4, y: 4, z: 16 (z_hi: 2, z_lo: 8; z = z_hi * 8 + z_lo), core: 2. Of those that a mesh axis runs over, the one named last changes fastest.
Arguments:
- strain: bfloat16 [2048, 640, 512], P('chan', 'freq'), may hold values from -120 to 120
- fiber_order: int32 [16, 128], P('chan'), may hold values from 0 to 127, each once within a row
- window_valid: int32 [2048, 640], P('chan', 'freq'), may hold values 0 or 1
- whiten: float32 [64], replicated, may hold values from 0.5 to 2
Outputs:
- cross_stack: float32 [64, 2, 9, 2048, 128], P('freq', None, None, 'chan')
The draws below stay inside these ranges and needn't reach their ends.
Inputs may be any that keep to these rules, and one draw needn't show every extreme that they name: Each row of fiber_order is a permutation of 0 to 127.
All inputs are finite; a program needn't handle non-finite values. No bound on the sum of `window_valid` on one device may be relied on, other than what follows from the above.
Results may differ from the reference program's by a relative error of at most 0.0054.
Values may be sent and summed in bfloat16 or wider, within the bound.
No kernel may reach another device: no remote copies, remote signals or barrier semaphores. Data moves between devices by JAX's collectives and lax.ppermute only.
A program may use at most 64 MiB of HBM per device.

```python
import math
import jax
import jax.numpy as jnp
from jax import lax

CH_DEV = 128
NT = 512
BIN0 = 8
BLOCKS = 16
CHANS = 2048
WINDOWS = 640
FREQS = 64
NOFF = 9


def draw_strain(key, part):
    noise_key, scale_key, offset_key = jax.random.split(key, 3)
    shape_full = (CHANS, WINDOWS, NT)
    scales = jnp.exp(jax.random.uniform(scale_key, (CHANS, WINDOWS, 1), jnp.float32, math.log(0.3), math.log(10.0)))
    drifts = jnp.clip(2.0 * jax.random.normal(offset_key, (CHANS, WINDOWS, 1), jnp.float32), -6.0, 6.0)
    noise = jnp.clip(jax.random.normal(noise_key, shape_full, jnp.float32), -6.0, 6.0)
    return (scales * (noise + drifts)).astype(jnp.bfloat16)


def with_ends(array, key, least, largest):
    extent = array.shape
    spot = [jax.random.randint(jax.random.fold_in(key, axis), (), 0, extent[axis]) for axis in range(len(extent))]
    array = array.at[tuple(spot)].set(least)
    longest = extent.index(max(extent))
    spot[longest] = (spot[longest] + 1) % extent[longest]
    return array.at[tuple(spot)].set(largest)


def setup_inputs(seed: int = 0) -> dict:
    streams_of = jax.random.split(jax.random.key(seed), 5)
    strain = draw_strain(jax.random.fold_in(streams_of[4], 71), 0)
    fiber_order = jax.vmap(lambda own: jax.random.permutation(own, CH_DEV))(jax.random.split(streams_of[1], BLOCKS)).reshape((BLOCKS, CH_DEV)).astype(jnp.int32)
    window_valid = with_ends((jax.random.randint(streams_of[2], (CHANS, WINDOWS), 0, 8) < 7).astype(jnp.int32), jax.random.fold_in(streams_of[2], 1), 0, 1)
    whiten = jnp.clip(jnp.exp(jax.random.uniform(streams_of[3], (FREQS,), jnp.float32, math.log(0.5), math.log(2.0))), 0.5, 2.0)
    return dict(strain=strain, fiber_order=fiber_order, window_valid=window_valid, whiten=whiten)


def fourier_table(frequency_count):
    sample_index = jnp.arange(NT, dtype=jnp.int32)
    bin_index = BIN0 + jnp.arange(frequency_count, dtype=jnp.int32)
    phase_index = sample_index[:, None] * bin_index[None, :] % NT
    angles = 2.0 * math.pi / NT * phase_index.astype(jnp.float32)
    hann_taper = 0.5 - 0.5 * jnp.cos(2.0 * math.pi / NT * sample_index.astype(jnp.float32))
    basis_table = jnp.stack([hann_taper[:, None] * jnp.cos(angles), -hann_taper[:, None] * jnp.sin(angles)], axis=2)
    return basis_table.reshape(NT, 2 * frequency_count).astype(jnp.bfloat16)

def normalize(ordered):
    widened = ordered.astype(jnp.float32)
    centered = widened - lax.optimization_barrier(jnp.mean(widened, axis=2, keepdims=True))
    power = lax.optimization_barrier(jnp.mean(centered * centered, axis=2, keepdims=True))
    return (centered * lax.rsqrt(power + 1e-06)).astype(jnp.bfloat16)

def reference(strain, fiber_order, window_valid, whiten):
    frequency_count = whiten.shape[0]
    basis_table = fourier_table(frequency_count)
    gain_pair = jnp.repeat(whiten, 2)
    norm_factor = 2.0 / math.sqrt(NT)

    def block_spectra(inputs):
        strain_block, order_row, valid_block = inputs
        ordered = jnp.take(strain_block, order_row, axis=0)
        live_flags = jnp.take(valid_block, order_row, axis=0)
        normed = normalize(ordered)
        spectra = jnp.einsum('cwt,tk->wkc', normed.astype(jnp.float32), basis_table.astype(jnp.float32))
        weights = jnp.transpose(live_flags).astype(jnp.float32)[:, None, :]
        return (spectra * gain_pair[None, :, None] * weights * norm_factor).astype(jnp.bfloat16)
    all_spectra = lax.map(block_spectra, (strain.reshape(BLOCKS, CH_DEV, WINDOWS, NT), fiber_order, window_valid.reshape(BLOCKS, CH_DEV, WINDOWS)))
    scale_back = 1.0 / math.sqrt(WINDOWS)

    def block_cross(source):
        left_side = all_spectra[source].astype(jnp.float32).reshape(WINDOWS, frequency_count, 2, CH_DEV)
        outputs = []
        for offset in range(NOFF):
            partner_index = ((source + offset) % BLOCKS).astype(jnp.int32)
            partner = lax.dynamic_index_in_dim(all_spectra, partner_index, 0, keepdims=False)
            partner = partner.astype(jnp.float32).reshape(WINDOWS, frequency_count, 2, CH_DEV)
            real_part = jnp.einsum('wkri,wkrj->kij', left_side, partner)
            imag_part = jnp.einsum('wki,wkj->kij', left_side[:, :, 1], partner[:, :, 0]) - jnp.einsum('wki,wkj->kij', left_side[:, :, 0], partner[:, :, 1])
            outputs.append(jnp.stack([real_part, imag_part], axis=1) * scale_back)
        return jnp.stack(outputs, axis=0)
    crossed = lax.map(block_cross, jnp.arange(BLOCKS, dtype=jnp.int32))
    return jnp.transpose(crossed, (2, 3, 1, 0, 4, 5)).reshape(frequency_count, 2, NOFF, CHANS, CH_DEV)
```

```python
import functools
import math

import jax
import jax.numpy as jnp
import numpy as np
from jax import lax
from jax.experimental import pallas as pl
from jax.experimental.pallas import tpu as pltpu
from jax.sharding import Mesh
from jax.sharding import PartitionSpec as P

CH = 128
NT = 512
BIN0 = 8
GROUP = 4
CHUNKS = (12, 8)
NOFF = 9


def basis_rows(groups):
    t = np.arange(NT)
    bins = BIN0 + np.arange(2 * groups)
    phase = (t[:, None] * bins[None, :] % NT).astype(np.float32)
    angles = np.float32(2.0 * math.pi / NT) * phase
    taper = np.float32(0.5) - np.float32(0.5) * np.cos(np.float32(2.0 * math.pi / NT) * t.astype(np.float32))
    table = np.stack([taper[:, None] * np.cos(angles), -taper[:, None] * np.sin(angles)], axis=2)
    table = table.reshape(NT, groups, 4).transpose(2, 1, 0).reshape(4 * groups, NT)
    return jnp.asarray(table.astype(jnp.bfloat16))


def spectra_body(strain, live, order, basis, gain, out, place, *, first, groups):
    step = pl.program_id(0)
    channel = lax.broadcasted_iota(jnp.int32, (CH, CH), 0)
    pick = (channel == order[...]).astype(jnp.float32).astype(jnp.bfloat16)
    for w in range(GROUP):
        value = strain[w].astype(jnp.float32)
        centered = value - jnp.sum(value, axis=1, keepdims=True) * (1.0 / NT)
        power = jnp.sum(centered * centered, axis=1, keepdims=True) * (1.0 / NT)
        normed = (centered * lax.rsqrt(power + 1e-06)).astype(jnp.bfloat16)
        spec = lax.dot_general(basis[...], normed, (((1,), (1,)), ((), ())), preferred_element_type=jnp.float32)
        weight = live[pl.ds(first + step * GROUP + w, 1), :].astype(jnp.float32)
        spec = (spec * gain[...] * weight).astype(jnp.bfloat16)
        spec = jnp.dot(spec, pick, preferred_element_type=jnp.float32)
        for part in range(4):
            place[pl.ds(part * GROUP + w, groups, stride=16), :] = spec[part * groups : (part + 1) * groups]
    packed = place[...].astype(jnp.bfloat16).reshape(4, groups // 4, 16, CH)
    out[:, 0] = packed
    out[:, 1] = packed


def spectra(strain, live, order, basis, gain, first, count):
    groups = basis.shape[0] // 4
    steps = count // GROUP
    base = first // GROUP
    return pl.pallas_call(
        functools.partial(spectra_body, first=first, groups=groups),
        grid=(steps,),
        in_specs=[
            pl.BlockSpec((GROUP, CH, NT), lambda i: (base + i, 0, 0)),
            pl.BlockSpec(live.shape, lambda i: (0, 0)),
            pl.BlockSpec((1, CH), lambda i: (0, 0)),
            pl.BlockSpec(basis.shape, lambda i: (0, 0)),
            pl.BlockSpec(gain.shape, lambda i: (0, 0)),
        ],
        out_specs=pl.BlockSpec((4, 2, groups // 4, 16, CH), lambda i: (0, 0, 0, i, 0)),
        out_shape=jax.ShapeDtypeStruct((4, 2, groups // 4, 4 * count, CH), jnp.bfloat16),
        scratch_shapes=[pltpu.VMEM((16 * groups, CH), jnp.float32)],
        name="spectra",
    )(strain, live, order, basis, gain)


def stack_body(where, *refs, chunks, scale):
    data, out = refs[: 6 * chunks], refs[6 * chunks]
    half, core = where[0], where[1]
    lefts = []
    for c in range(chunks):
        own = data[6 * c][:, half]
        own = own.reshape(-1, 8, CH).astype(jnp.float32)
        turned = pltpu.roll(own, 4, 1)
        part = lax.broadcasted_iota(jnp.int32, own.shape, 1)
        turned = jnp.where(part < 4, turned, -turned)
        own = own.reshape(-1, CH).T
        turned = turned.reshape(-1, CH).T
        which = lax.broadcasted_iota(jnp.int32, own.shape, 1) % 16 < 8
        zero = jnp.zeros_like(own)
        left = [
            jnp.where(which, own, zero),
            jnp.where(which, turned, zero),
            jnp.where(which, zero, own),
            jnp.where(which, zero, turned),
        ]
        lefts.append(jnp.concatenate([v.astype(jnp.bfloat16) for v in left], axis=0))
    for ahead in range(3):
        for other in range(2):
            total = None
            for c in range(chunks):
                ref = data[6 * c + 3 * other + ahead]
                right = jnp.concatenate([ref[:, 0].reshape(-1, CH), ref[:, 1].reshape(-1, CH)], axis=1)
                term = jnp.dot(lefts[c], right, preferred_element_type=jnp.float32)
                total = term if total is None else total + term
            total = total * scale
            for side in range(2):
                offset = 4 * ahead + 2 * (side - half) + other * (1 - 2 * core)

                @pl.when(jnp.logical_and(offset >= 0, offset < NOFF))
                def _(total=total, side=side, offset=offset):
                    for k in range(2):
                        for s in range(2):
                            row = (2 * k + s) * CH
                            out[k, s, offset] = total[row : row + CH, side * CH : (side + 1) * CH]


def stack(where, data, chunks, scale):
    whole = pl.BlockSpec(memory_space=pltpu.VMEM)
    return pl.pallas_call(
        functools.partial(stack_body, chunks=chunks, scale=scale),
        in_specs=[pl.BlockSpec(memory_space=pltpu.SMEM)] + [whole] * len(data),
        out_specs=whole,
        out_shape=jax.ShapeDtypeStruct((2, 2, NOFF, CH, CH), jnp.float32),
        compiler_params=pltpu.CompilerParams(vmem_limit_bytes=56 * 1024 * 1024),
        name="stack",
    )(where, *data)


def shifted(value, axis, steps):
    count = lax.axis_size(axis)
    return lax.ppermute(value, axis, [(s, (s + steps) % count) for s in range(count)])


def local(strain, fiber_order, window_valid, whiten):
    groups = whiten.shape[0] // 2
    windows = strain.shape[1]
    strain = jnp.transpose(strain, (1, 0, 2))
    live = jnp.transpose(window_valid)
    basis = basis_rows(groups)
    gain = whiten.reshape(groups, 2).T * (2.0 / math.sqrt(NT))
    gain = jnp.repeat(gain, 2, axis=0).reshape(4 * groups, 1)
    where = jnp.stack([lax.axis_index("z_hi"), lax.axis_index("core")]).astype(jnp.int32)
    data = []
    first = 0
    for count in CHUNKS:
        sent = spectra(strain, live, fiber_order, basis, gain, first, count)
        first += count
        here = lax.all_to_all(sent.reshape(2 * groups, 4 * count, CH), ("x", "z_hi", "z_lo"), 0, 0, tiled=True)
        here = here.reshape(4, 2, groups // 4, 4 * count, CH)
        ahead1 = shifted(here, "y", -1)
        ahead2 = shifted(shifted(here, "y", 1), "y", 1)
        own = [here, ahead1, ahead2]
        data += own + [shifted(v, "core", 1) for v in own]
    total = windows * lax.axis_size("x") * lax.axis_size("z_lo")
    return stack(where, [v.reshape(4, 2, -1, CH) for v in data], len(CHUNKS), 1.0 / math.sqrt(total))


def solution(mesh):
    fine = Mesh(mesh.devices.reshape(4, 8, 4, 2, 2), ("x", "z_lo", "y", "z_hi", "core"))
    freq, chan = ("x", "z_lo"), ("y", "z_hi", "core")
    in_specs = (P(chan, freq, None), P(chan, None), P(chan, freq), P())
    out_specs = P(freq, None, None, chan, None)
    return jax.shard_map(local, mesh=fine, in_specs=in_specs, out_specs=out_specs, check_vma=False)
```

```python
import functools
import math

import jax
import jax.numpy as jnp
import numpy as np
from jax import lax
from jax.experimental import pallas as pl
from jax.experimental.pallas import tpu as pltpu
from jax.sharding import Mesh
from jax.sharding import PartitionSpec as P

CH = 128
NT = 512
BIN0 = 8
GROUP = 2
CHUNKS = (14, 6)
NOFF = 9
VMEM = pltpu.CompilerParams(vmem_limit_bytes=48 * 1024 * 1024)


def basis_rows(groups):
    t = np.arange(NT)
    bins = BIN0 + np.arange(2 * groups)
    phase = (t[:, None] * bins[None, :] % NT).astype(np.float32)
    angles = np.float32(2.0 * math.pi / NT) * phase
    taper = np.float32(0.5) - np.float32(0.5) * np.cos(np.float32(2.0 * math.pi / NT) * t.astype(np.float32))
    table = np.stack([taper[:, None] * np.cos(angles), -taper[:, None] * np.sin(angles)], axis=2)
    table = table.reshape(NT, groups, 4).transpose(2, 1, 0).reshape(4 * groups, NT)
    return jnp.asarray(table.astype(jnp.bfloat16))


def spectra_body(strain, live, order, basis, whiten, out, place, *, first, groups, rows):
    step = pl.program_id(0)
    channel = lax.broadcasted_iota(jnp.int32, (CH, CH), 0)
    pick = (channel == order[...]).astype(jnp.float32).astype(jnp.bfloat16)
    shape = (4 * groups, 2 * groups)
    row = lax.broadcasted_iota(jnp.int32, shape, 0)
    column = lax.broadcasted_iota(jnp.int32, shape, 1)
    spread = jnp.where(column == 2 * (row % groups) + row // (2 * groups), whiten[...], 0.0)
    gain = jnp.sum(spread, axis=1, keepdims=True) * (2.0 / math.sqrt(NT))
    for w in range(GROUP):
        at = step * GROUP + w
        value = strain[w].astype(jnp.float32)
        centered = value - jnp.sum(value, axis=1, keepdims=True) * (1.0 / NT)
        power = jnp.sum(centered * centered, axis=1, keepdims=True) * (1.0 / NT)
        normed = (centered * lax.rsqrt(power + 1e-06)).astype(jnp.bfloat16)
        spec = lax.dot_general(basis[...], normed, (((1,), (1,)), ((), ())), preferred_element_type=jnp.float32)
        weight = live[pl.ds(first + at, 1), :].astype(jnp.float32)
        spec = (spec * gain * weight).astype(jnp.bfloat16)
        spec = jnp.dot(spec, pick, preferred_element_type=jnp.float32)
        for part in range(4):
            place[pl.ds(at * 4 + part, groups, stride=rows), :] = spec[part * groups : (part + 1) * groups]

    @pl.when(step == pl.num_programs(0) - 1)
    def _():
        for x in range(4):
            size = groups * rows // 4
            packed = place[x * size : (x + 1) * size].astype(jnp.bfloat16)
            out[x, 0] = packed
            out[x, 1] = packed


def spectra(strain, live, order, basis, whiten, first, count):
    groups = basis.shape[0] // 4
    base = first // GROUP
    rows = 4 * count
    shape = (4, 2, groups * rows // 4, CH)
    whole = lambda v: pl.BlockSpec(v.shape, lambda i: (0,) * v.ndim)
    return pl.pallas_call(
        functools.partial(spectra_body, first=first, groups=groups, rows=rows),
        grid=(count // GROUP,),
        in_specs=[
            pl.BlockSpec((GROUP, CH, NT), lambda i: (base + i, 0, 0)),
            whole(live),
            whole(order),
            whole(basis),
            whole(whiten),
        ],
        out_specs=pl.BlockSpec(shape, lambda i: (0, 0, 0, 0)),
        out_shape=jax.ShapeDtypeStruct(shape, jnp.bfloat16),
        scratch_shapes=[pltpu.VMEM((groups * rows, CH), jnp.float32)],
        compiler_params=VMEM,
        name="spectra",
    )(strain, live, order, basis, whiten)


def left_body(where, data, out):
    own = data[:, where[0]]
    own = own.reshape(-1, CH).astype(jnp.float32)
    own = own.reshape(-1, 8, CH)
    part = lax.broadcasted_iota(jnp.int32, own.shape, 1)
    turned = jnp.where(part % 2 == 0, pltpu.roll(own, 7, 1), -pltpu.roll(own, 1, 1))
    own = own.reshape(-1, CH).T
    turned = turned.reshape(-1, CH).T
    first = lax.broadcasted_iota(jnp.int32, own.shape, 1) % 4 < 2
    zero = jnp.zeros_like(own)
    out[0 * CH : 1 * CH] = jnp.where(first, own, zero).astype(jnp.bfloat16)
    out[1 * CH : 2 * CH] = jnp.where(first, turned, zero).astype(jnp.bfloat16)
    out[2 * CH : 3 * CH] = jnp.where(first, zero, own).astype(jnp.bfloat16)
    out[3 * CH : 4 * CH] = jnp.where(first, zero, turned).astype(jnp.bfloat16)


def left_of(where, data):
    whole = pl.BlockSpec(memory_space=pltpu.VMEM)
    return pl.pallas_call(
        left_body,
        in_specs=[pl.BlockSpec(memory_space=pltpu.SMEM), whole],
        out_specs=whole,
        out_shape=jax.ShapeDtypeStruct((4 * CH, data.shape[0] * data.shape[2]), jnp.bfloat16),
        compiler_params=VMEM,
        name="left",
    )(where, data)


def product(left, ref):
    right = jnp.concatenate([ref[:, 0].reshape(-1, CH), ref[:, 1].reshape(-1, CH)], axis=1)
    return jnp.dot(left[...], right, preferred_element_type=jnp.float32)


def early_body(left, *refs):
    data, out = refs[:-1], refs[-1]
    for i, ref in enumerate(data):
        out[i] = product(left, ref)


def early(left, data):
    whole = pl.BlockSpec(memory_space=pltpu.VMEM)
    return pl.pallas_call(
        early_body,
        in_specs=[whole] * (1 + len(data)),
        out_specs=whole,
        out_shape=jax.ShapeDtypeStruct((len(data), 4 * CH, 2 * CH), jnp.float32),
        compiler_params=VMEM,
        name="early",
    )(left, *data)


def late_body(where, left, begun, one, two, *refs, ahead, scale):
    out, stage, done = refs[-3:]
    half, core = where[0], where[1]
    jobs = []
    for other, ref in enumerate((one, two)):
        total = (begun[other] + product(left, ref)) * scale
        for side in range(2):
            spot = 2 * other + side
            for part in range(4):
                row = part * CH
                stage[spot, part // 2, part % 2] = total[row : row + CH, side * CH : (side + 1) * CH]
            offset = 4 * ahead + 2 * (side - half) + other * (1 - 2 * core)
            valid = jnp.logical_and(offset >= 0, offset < NOFF)
            target = jnp.clip(offset, 0, NOFF - 1)
            copy = pltpu.make_async_copy(stage.at[spot], out.at[:, :, target], done.at[spot])
            jobs.append((valid, copy))
            pl.when(valid)(copy.start)
    for valid, copy in jobs:
        pl.when(valid)(copy.wait)


def late(where, left, begun, one, two, filled, ahead, scale):
    whole = pl.BlockSpec(memory_space=pltpu.VMEM)
    somewhere = pl.BlockSpec(memory_space=pl.ANY)
    extra = [] if filled is None else [filled]
    return pl.pallas_call(
        functools.partial(late_body, ahead=ahead, scale=scale),
        grid=(1,),
        in_specs=[
            pl.BlockSpec(memory_space=pltpu.SMEM),
            whole,
            pl.BlockSpec((2, 4 * CH, 2 * CH), lambda i: (ahead, 0, 0)),
            whole,
            whole,
        ]
        + [somewhere] * len(extra),
        out_specs=somewhere,
        out_shape=jax.ShapeDtypeStruct((2, 2, NOFF, CH, CH), jnp.float32),
        input_output_aliases={5: 0} if extra else {},
        scratch_shapes=[pltpu.VMEM((4, 2, 2, CH, CH), jnp.float32), pltpu.SemaphoreType.DMA((4,))],
        compiler_params=VMEM,
        name="late",
    )(where, left, begun, one, two, *extra)


def shifted(value, axis, steps):
    count = lax.axis_size(axis)
    return lax.ppermute(value, axis, [(s, (s + steps) % count) for s in range(count)])


def upper(value, steps):
    count = lax.axis_size("y")
    pairs = [(2 * y + 1, 2 * ((y + steps) % count) + 1) for y in range(count)]
    return lax.ppermute(value, ("y", "z_hi"), pairs)


def neighbours(here):
    ahead1 = shifted(here, "y", -1)
    ahead2 = jnp.stack([shifted(shifted(here[:, 0], "y", 1), "y", 1), upper(here[:, 1], 2)], axis=1)
    own = [here, ahead1, ahead2]
    return [w for v in own for w in (v, shifted(v, "core", 1))]


def local(strain, fiber_order, window_valid, whiten):
    groups = whiten.shape[0] // 2
    windows = strain.shape[1]
    strain = jnp.transpose(strain, (1, 0, 2))
    live = jnp.transpose(window_valid)
    basis = basis_rows(groups)
    where = jnp.stack([lax.axis_index("z_hi"), lax.axis_index("core")]).astype(jnp.int32)
    scale = 1.0 / math.sqrt(windows * lax.axis_size("x") * lax.axis_size("z_lo"))

    def made(first, count):
        sent = spectra(strain, live, fiber_order, basis, whiten.reshape(1, -1), first, count)
        return sent.reshape(2 * groups, 4 * count, CH)

    def spread(sent):
        here = lax.all_to_all(sent, ("x", "z_hi", "z_lo"), 0, 0, tiled=True)
        return here.reshape(4, 2, -1, CH)

    first, second = spread(made(0, CHUNKS[0])), made(*CHUNKS)
    first, second = lax.optimization_barrier((first, second))
    head = neighbours(first)
    tail = spread(second)
    tail, *head = lax.optimization_barrier((tail, *head))
    rest = neighbours(tail)
    begun = early(left_of(where, head[0]), head)
    left = left_of(where, tail)
    filled = None
    for ahead in range(3):
        one, two = rest[2 * ahead : 2 * ahead + 2]
        filled = late(where, left, begun, one, two, filled, ahead, scale)
    return filled


def solution(mesh):
    fine = Mesh(mesh.devices.reshape(4, 8, 4, 2, 2), ("x", "z_lo", "y", "z_hi", "core"))
    freq, chan = ("x", "z_lo"), ("y", "z_hi", "core")
    in_specs = (P(chan, freq, None), P(chan, None), P(chan, freq), P())
    out_specs = P(freq, None, None, chan, None)
    return jax.shard_map(local, mesh=fine, in_specs=in_specs, out_specs=out_specs, check_vma=False)
```

```python
import functools
import math

import jax
import jax.numpy as jnp
import numpy as np
from jax import lax
from jax.experimental import pallas as pl
from jax.experimental.pallas import tpu as pltpu
from jax.sharding import Mesh
from jax.sharding import PartitionSpec as P

CH = 128
NT = 512
BIN0 = 8
GROUP = 2
CHUNKS = (14, 6)
NOFF = 9


def grant(mib):
    return pltpu.CompilerParams(vmem_limit_bytes=mib * 1024 * 1024)


def basis_rows(groups):
    t = np.arange(NT)
    bins = BIN0 + np.arange(2 * groups)
    phase = (t[:, None] * bins[None, :] % NT).astype(np.float32)
    angles = np.float32(2.0 * math.pi / NT) * phase
    taper = np.float32(0.5) - np.float32(0.5) * np.cos(np.float32(2.0 * math.pi / NT) * t.astype(np.float32))
    table = np.stack([taper[:, None] * np.cos(angles), -taper[:, None] * np.sin(angles)], axis=2)
    table = table.reshape(NT, groups, 4).transpose(2, 1, 0).reshape(4 * groups, NT)
    return jnp.asarray(table.astype(jnp.bfloat16))


def spectra_body(strain, live, order, basis, whiten, out, place, *, first, groups, rows):
    step = pl.program_id(0)
    channel = lax.broadcasted_iota(jnp.int32, (CH, CH), 0)
    pick = (channel == order[...]).astype(jnp.float32).astype(jnp.bfloat16)
    shape = (4 * groups, 2 * groups)
    row = lax.broadcasted_iota(jnp.int32, shape, 0)
    column = lax.broadcasted_iota(jnp.int32, shape, 1)
    spread = jnp.where(column == 2 * (row % groups) + row // (2 * groups), whiten[...], 0.0)
    gain = jnp.sum(spread, axis=1, keepdims=True) * (2.0 / math.sqrt(NT))
    for w in range(GROUP):
        at = step * GROUP + w
        value = strain[w].astype(jnp.float32)
        centered = value - jnp.sum(value, axis=1, keepdims=True) * (1.0 / NT)
        power = jnp.sum(centered * centered, axis=1, keepdims=True) * (1.0 / NT)
        normed = (centered * lax.rsqrt(power + 1e-06)).astype(jnp.bfloat16)
        spec = lax.dot_general(basis[...], normed, (((1,), (1,)), ((), ())), preferred_element_type=jnp.float32)
        weight = live[pl.ds(first + at, 1), :].astype(jnp.float32)
        spec = (spec * gain * weight).astype(jnp.bfloat16)
        spec = jnp.dot(spec, pick, preferred_element_type=jnp.float32)
        for part in range(4):
            place[pl.ds(at * 4 + part, groups, stride=rows), :] = spec[part * groups : (part + 1) * groups]

    @pl.when(step == pl.num_programs(0) - 1)
    def _():
        for x in range(4):
            size = groups * rows // 4
            packed = place[x * size : (x + 1) * size].astype(jnp.bfloat16)
            out[x, 0] = packed
            out[x, 1] = packed


def spectra(strain, live, order, basis, whiten, first, count):
    groups = basis.shape[0] // 4
    base = first // GROUP
    rows = 4 * count
    shape = (4, 2, groups * rows // 4, CH)
    whole = lambda v: pl.BlockSpec(v.shape, lambda i: (0,) * v.ndim)
    return pl.pallas_call(
        functools.partial(spectra_body, first=first, groups=groups, rows=rows),
        grid=(count // GROUP,),
        in_specs=[
            pl.BlockSpec((GROUP, CH, NT), lambda i: (base + i, 0, 0)),
            whole(live),
            whole(order),
            whole(basis),
            whole(whiten),
        ],
        out_specs=pl.BlockSpec(shape, lambda i: (0, 0, 0, 0)),
        out_shape=jax.ShapeDtypeStruct(shape, jnp.bfloat16),
        scratch_shapes=[pltpu.VMEM((groups * rows, CH), jnp.float32)],
        name="spectra",
    )(strain, live, order, basis, whiten)


def left_body(where, data, out):
    own = data[:, where[0]]
    own = own.reshape(-1, CH).astype(jnp.float32)
    own = own.reshape(-1, 8, CH)
    part = lax.broadcasted_iota(jnp.int32, own.shape, 1)
    turned = jnp.where(part % 2 == 0, pltpu.roll(own, 7, 1), -pltpu.roll(own, 1, 1))
    own = own.reshape(-1, CH).T
    turned = turned.reshape(-1, CH).T
    first = lax.broadcasted_iota(jnp.int32, own.shape, 1) % 4 < 2
    zero = jnp.zeros_like(own)
    out[0 * CH : 1 * CH] = jnp.where(first, own, zero).astype(jnp.bfloat16)
    out[1 * CH : 2 * CH] = jnp.where(first, turned, zero).astype(jnp.bfloat16)
    out[2 * CH : 3 * CH] = jnp.where(first, zero, own).astype(jnp.bfloat16)
    out[3 * CH : 4 * CH] = jnp.where(first, zero, turned).astype(jnp.bfloat16)


def left_of(where, data):
    whole = pl.BlockSpec(memory_space=pltpu.VMEM)
    return pl.pallas_call(
        left_body,
        in_specs=[pl.BlockSpec(memory_space=pltpu.SMEM), whole],
        out_specs=whole,
        out_shape=jax.ShapeDtypeStruct((4 * CH, data.shape[0] * data.shape[2]), jnp.bfloat16),
        compiler_params=grant(12),
        name="left",
    )(where, data)


def product(left, ref):
    right = jnp.concatenate([ref[:, 0].reshape(-1, CH), ref[:, 1].reshape(-1, CH)], axis=1)
    return jnp.dot(left[...], right, preferred_element_type=jnp.float32)


def early_body(left, *refs):
    for i in range(6):
        refs[6 + i // 2][i % 2] = product(left, refs[i])


def early(left, data):
    whole = pl.BlockSpec(memory_space=pltpu.VMEM)
    return pl.pallas_call(
        early_body,
        in_specs=[whole] * 7,
        out_specs=[whole] * 3,
        out_shape=[jax.ShapeDtypeStruct((2, 4 * CH, 2 * CH), jnp.float32)] * 3,
        cost_estimate=pl.CostEstimate(flops=7 * 10**9, transcendentals=0, bytes_accessed=12 * 10**6),
        compiler_params=grant(24),
        name="early",
    )(left, *data)


def late_body(where, left, begun, one, two, *refs, ahead, scale):
    out, stage, done = refs[-3:]
    half, core = where[0], where[1]
    jobs = []
    for other, ref in enumerate((one, two)):
        total = (begun[other] + product(left, ref)) * scale
        for side in range(2):
            spot = 2 * other + side
            for part in range(4):
                row = part * CH
                stage[spot, part // 2, part % 2] = total[row : row + CH, side * CH : (side + 1) * CH]
            offset = 4 * ahead + 2 * (side - half) + other * (1 - 2 * core)
            valid = jnp.logical_and(offset >= 0, offset < NOFF)
            target = jnp.clip(offset, 0, NOFF - 1)
            copy = pltpu.make_async_copy(stage.at[spot], out.at[:, :, target], done.at[spot])
            jobs.append((valid, copy))
            pl.when(valid)(copy.start)
    for valid, copy in jobs:
        pl.when(valid)(copy.wait)


def late(where, left, begun, one, two, filled, ahead, scale):
    whole = pl.BlockSpec(memory_space=pltpu.VMEM)
    somewhere = pl.BlockSpec(memory_space=pl.ANY)
    extra = [] if filled is None else [filled]
    return pl.pallas_call(
        functools.partial(late_body, ahead=ahead, scale=scale),
        in_specs=[
            pl.BlockSpec(memory_space=pltpu.SMEM),
            whole,
            whole,
            whole,
            whole,
        ]
        + [somewhere] * len(extra),
        out_specs=somewhere,
        out_shape=jax.ShapeDtypeStruct((2, 2, NOFF, CH, CH), jnp.float32),
        input_output_aliases={5: 0} if extra else {},
        scratch_shapes=[pltpu.VMEM((4, 2, 2, CH, CH), jnp.float32), pltpu.SemaphoreType.DMA((4,))],
        cost_estimate=pl.CostEstimate(flops=2 * 10**9, transcendentals=0, bytes_accessed=4 * 10**6),
        compiler_params=grant(16),
        name="late",
    )(where, left, begun, one, two, *extra)


def shifted(value, axis, steps):
    count = lax.axis_size(axis)
    return lax.ppermute(value, axis, [(s, (s + steps) % count) for s in range(count)])


def upper(value, steps):
    count = lax.axis_size("y")
    pairs = [(2 * y + 1, 2 * ((y + steps) % count) + 1) for y in range(count)]
    return lax.ppermute(value, ("y", "z_hi"), pairs)


def fetched(here, direct):
    ahead1 = shifted(here, "y", -1)
    if direct:
        low = shifted(here[:, 0], "y", 2)
    else:
        low = shifted(shifted(here[:, 0], "y", 1), "y", 1)
    return [here, ahead1, jnp.stack([low, upper(here[:, 1], 2)], axis=1)]


def both(own):
    return [w for v in own for w in (v, shifted(v, "core", 1))]


def local(strain, fiber_order, window_valid, whiten):
    groups = whiten.shape[0] // 2
    windows = strain.shape[1]
    strain = jnp.transpose(strain, (1, 0, 2))
    live = jnp.transpose(window_valid)
    basis = basis_rows(groups)
    where = jnp.stack([lax.axis_index("z_hi"), lax.axis_index("core")]).astype(jnp.int32)
    scale = 1.0 / math.sqrt(windows * lax.axis_size("x") * lax.axis_size("z_lo"))

    def made(first, count):
        sent = spectra(strain, live, fiber_order, basis, whiten.reshape(1, -1), first, count)
        return sent.reshape(2 * groups, 4 * count, CH)

    def spread(sent):
        here = lax.all_to_all(sent, ("x", "z_hi", "z_lo"), 0, 0, tiled=True)
        return here.reshape(4, 2, -1, CH)

    first, second = spread(made(0, CHUNKS[0])), made(*CHUNKS)
    first, second = lax.optimization_barrier((first, second))
    head = both(fetched(first, False))
    tail = spread(second)
    tail, *head = lax.optimization_barrier((tail, *head))
    rest = fetched(tail, True)
    crossed = shifted(tail, "core", 1)
    begun = early(left_of(where, head[0]), head)
    left = left_of(where, tail)
    *rest, crossed, left, begun = lax.optimization_barrier((*rest[1:], crossed, left, begun))
    rest = [tail, crossed, *both(rest)]
    filled = None
    for ahead in range(3):
        one, two = rest[2 * ahead : 2 * ahead + 2]
        filled = late(where, left, begun[ahead], one, two, filled, ahead, scale)
    return filled


def solution(mesh):
    fine = Mesh(mesh.devices.reshape(4, 8, 4, 2, 2), ("x", "z_lo", "y", "z_hi", "core"))
    freq, chan = ("x", "z_lo"), ("y", "z_hi", "core")
    in_specs = (P(chan, freq, None), P(chan, None), P(chan, freq), P())
    out_specs = P(freq, None, None, chan, None)
    return jax.shard_map(local, mesh=fine, in_specs=in_specs, out_specs=out_specs, check_vma=False)
```

```python
import functools
import math

import jax
import jax.numpy as jnp
import numpy as np
from jax import lax
from jax.experimental import pallas as pl
from jax.experimental.pallas import tpu as pltpu
from jax.sharding import Mesh
from jax.sharding import PartitionSpec as P

CH = 128
NT = 512
BIN0 = 8
GROUP = 2
CHUNKS = (14, 6)
NOFF = 9


def grant(mib):
    return pltpu.CompilerParams(vmem_limit_bytes=mib * 1024 * 1024)


def basis_rows(groups):
    t = np.arange(NT)
    bins = BIN0 + np.arange(2 * groups)
    phase = (t[:, None] * bins[None, :] % NT).astype(np.float32)
    angles = np.float32(2.0 * math.pi / NT) * phase
    taper = np.float32(0.5) - np.float32(0.5) * np.cos(np.float32(2.0 * math.pi / NT) * t.astype(np.float32))
    table = np.stack([taper[:, None] * np.cos(angles), -taper[:, None] * np.sin(angles)], axis=2)
    table = table.reshape(NT, groups, 4).transpose(2, 1, 0).reshape(4 * groups, NT)
    return jnp.asarray(table.astype(jnp.bfloat16))


def spectra_body(strain, live, order, basis, whiten, out, held, place, loaded, *, first, count, groups):
    rows = 4 * count

    def load(i):
        part = pl.ds(first + i * GROUP, GROUP)
        return pltpu.make_async_copy(strain.at[part], held.at[pl.ds(i * GROUP, GROUP)], loaded.at[i])

    for i in range(count // GROUP):
        load(i).start()
    channel = lax.broadcasted_iota(jnp.int32, (CH, CH), 0)
    pick = (channel == order[...]).astype(jnp.float32).astype(jnp.bfloat16)
    shape = (4 * groups, 2 * groups)
    row = lax.broadcasted_iota(jnp.int32, shape, 0)
    column = lax.broadcasted_iota(jnp.int32, shape, 1)
    spread = jnp.where(column == 2 * (row % groups) + row // (2 * groups), whiten[...], 0.0)
    gain = jnp.sum(spread, axis=1, keepdims=True) * (2.0 / math.sqrt(NT))
    for i in range(count // GROUP):
        load(i).wait()
        for at in range(i * GROUP, (i + 1) * GROUP):
            value = held[at].astype(jnp.float32)
            centered = value - jnp.sum(value, axis=1, keepdims=True) * (1.0 / NT)
            power = jnp.sum(centered * centered, axis=1, keepdims=True) * (1.0 / NT)
            normed = (centered * lax.rsqrt(power + 1e-06)).astype(jnp.bfloat16)
            spec = lax.dot_general(basis[...], normed, (((1,), (1,)), ((), ())), preferred_element_type=jnp.float32)
            weight = live[first + at : first + at + 1, :].astype(jnp.float32)
            spec = (spec * gain * weight).astype(jnp.bfloat16)
            spec = jnp.dot(spec, pick, preferred_element_type=jnp.float32)
            for part in range(4):
                place[pl.ds(at * 4 + part, groups, stride=rows), :] = spec[part * groups : (part + 1) * groups]
    for x in range(4):
        size = groups * rows // 4
        packed = place[x * size : (x + 1) * size].astype(jnp.bfloat16)
        out[x, 0] = packed
        out[x, 1] = packed


def spectra(strain, live, order, basis, whiten, first, count):
    groups = basis.shape[0] // 4
    rows = 4 * count
    whole = pl.BlockSpec(memory_space=pltpu.VMEM)
    return pl.pallas_call(
        functools.partial(spectra_body, first=first, count=count, groups=groups),
        in_specs=[pl.BlockSpec(memory_space=pl.ANY)] + [whole] * 4,
        out_specs=whole,
        out_shape=jax.ShapeDtypeStruct((4, 2, groups * rows // 4, CH), jnp.bfloat16),
        scratch_shapes=[
            pltpu.VMEM((count, CH, NT), jnp.bfloat16),
            pltpu.VMEM((groups * rows, CH), jnp.float32),
            pltpu.SemaphoreType.DMA((count // GROUP,)),
        ],
        name="spectra",
    )(strain, live, order, basis, whiten)


def left_body(where, data, out):
    own = data[:, where[0]]
    own = own.reshape(-1, CH).astype(jnp.float32)
    own = own.reshape(-1, 8, CH)
    part = lax.broadcasted_iota(jnp.int32, own.shape, 1)
    turned = jnp.where(part % 2 == 0, pltpu.roll(own, 7, 1), -pltpu.roll(own, 1, 1))
    own = own.reshape(-1, CH).T
    turned = turned.reshape(-1, CH).T
    first = lax.broadcasted_iota(jnp.int32, own.shape, 1) % 4 < 2
    zero = jnp.zeros_like(own)
    out[0 * CH : 1 * CH] = jnp.where(first, own, zero).astype(jnp.bfloat16)
    out[1 * CH : 2 * CH] = jnp.where(first, turned, zero).astype(jnp.bfloat16)
    out[2 * CH : 3 * CH] = jnp.where(first, zero, own).astype(jnp.bfloat16)
    out[3 * CH : 4 * CH] = jnp.where(first, zero, turned).astype(jnp.bfloat16)


def left_of(where, data):
    whole = pl.BlockSpec(memory_space=pltpu.VMEM)
    return pl.pallas_call(
        left_body,
        in_specs=[pl.BlockSpec(memory_space=pltpu.SMEM), whole],
        out_specs=whole,
        out_shape=jax.ShapeDtypeStruct((4 * CH, data.shape[0] * data.shape[2]), jnp.bfloat16),
        compiler_params=grant(12),
        name="left",
    )(where, data)


def product(left, ref):
    right = jnp.concatenate([ref[:, 0].reshape(-1, CH), ref[:, 1].reshape(-1, CH)], axis=1)
    return jnp.dot(left[...], right, preferred_element_type=jnp.float32)


def early_body(left, *refs):
    for i in range(6):
        refs[6 + i // 2][i % 2] = product(left, refs[i])


def early(left, data):
    whole = pl.BlockSpec(memory_space=pltpu.VMEM)
    return pl.pallas_call(
        early_body,
        in_specs=[whole] * 7,
        out_specs=[whole] * 3,
        out_shape=[jax.ShapeDtypeStruct((2, 4 * CH, 2 * CH), jnp.float32)] * 3,
        cost_estimate=pl.CostEstimate(flops=7 * 10**9, transcendentals=0, bytes_accessed=12 * 10**6),
        compiler_params=grant(24),
        name="early",
    )(left, *data)


def late_body(where, left, begun, one, two, *refs, ahead, scale):
    out, stage, done = refs[-3:]
    half, core = where[0], where[1]
    jobs = []
    for other, ref in enumerate((one, two)):
        total = (begun[other] + product(left, ref)) * scale
        for side in range(2):
            spot = 2 * other + side
            for part in range(4):
                row = part * CH
                stage[spot, part // 2, part % 2] = total[row : row + CH, side * CH : (side + 1) * CH]
            offset = 4 * ahead + 2 * (side - half) + other * (1 - 2 * core)
            valid = jnp.logical_and(offset >= 0, offset < NOFF)
            target = jnp.clip(offset, 0, NOFF - 1)
            copy = pltpu.make_async_copy(stage.at[spot], out.at[:, :, target], done.at[spot])
            jobs.append((valid, copy))
            pl.when(valid)(copy.start)
    for valid, copy in jobs:
        pl.when(valid)(copy.wait)


def late(where, left, begun, one, two, filled, ahead, scale):
    whole = pl.BlockSpec(memory_space=pltpu.VMEM)
    somewhere = pl.BlockSpec(memory_space=pl.ANY)
    extra = [] if filled is None else [filled]
    return pl.pallas_call(
        functools.partial(late_body, ahead=ahead, scale=scale),
        in_specs=[
            pl.BlockSpec(memory_space=pltpu.SMEM),
            whole,
            whole,
            whole,
            whole,
        ]
        + [somewhere] * len(extra),
        out_specs=somewhere,
        out_shape=jax.ShapeDtypeStruct((2, 2, NOFF, CH, CH), jnp.float32),
        input_output_aliases={5: 0} if extra else {},
        scratch_shapes=[pltpu.VMEM((4, 2, 2, CH, CH), jnp.float32), pltpu.SemaphoreType.DMA((4,))],
        cost_estimate=pl.CostEstimate(flops=2 * 10**9, transcendentals=0, bytes_accessed=4 * 10**6),
        compiler_params=grant(16),
        name="late",
    )(where, left, begun, one, two, *extra)


def shifted(value, axis, steps):
    count = lax.axis_size(axis)
    return lax.ppermute(value, axis, [(s, (s + steps) % count) for s in range(count)])


def fetched(here):
    return [here, shifted(here, "y", -1), shifted(here, "y", 2)]


def both(own):
    return [w for v in own for w in (v, shifted(v, "core", 1))]


def local(strain, fiber_order, window_valid, whiten):
    groups = whiten.shape[0] // 2
    windows = strain.shape[1]
    strain = jnp.transpose(strain, (1, 0, 2))
    live = jnp.transpose(window_valid)
    basis = basis_rows(groups)
    where = jnp.stack([lax.axis_index("z_hi"), lax.axis_index("core")]).astype(jnp.int32)
    scale = 1.0 / math.sqrt(windows * lax.axis_size("x") * lax.axis_size("z_lo"))

    def made(first, count):
        sent = spectra(strain, live, fiber_order, basis, whiten.reshape(1, -1), first, count)
        return sent.reshape(2 * groups, 4 * count, CH)

    def spread(sent):
        here = lax.all_to_all(sent, ("x", "z_hi", "z_lo"), 0, 0, tiled=True)
        return here.reshape(4, 2, -1, CH)

    first, second = spread(made(0, CHUNKS[0])), made(*CHUNKS)
    first, second = lax.optimization_barrier((first, second))
    head = both(fetched(first))
    tail = spread(second)
    tail, *head = lax.optimization_barrier((tail, *head))
    rest = fetched(tail)
    crossed = shifted(tail, "core", 1)
    begun = early(left_of(where, head[0]), head)
    left = left_of(where, tail)
    *rest, crossed, left, begun = lax.optimization_barrier((*rest[1:], crossed, left, begun))
    rest = [tail, crossed, *both(rest)]
    filled = None
    for ahead in range(3):
        one, two = rest[2 * ahead : 2 * ahead + 2]
        filled = late(where, left, begun[ahead], one, two, filled, ahead, scale)
    return filled


def solution(mesh):
    fine = Mesh(mesh.devices.reshape(4, 8, 4, 2, 2), ("x", "z_lo", "y", "z_hi", "core"))
    freq, chan = ("x", "z_lo"), ("y", "z_hi", "core")
    in_specs = (P(chan, freq, None), P(chan, None), P(chan, freq), P())
    out_specs = P(freq, None, None, chan, None)
    return jax.shard_map(local, mesh=fine, in_specs=in_specs, out_specs=out_specs, check_vma=False)
```

```python
import functools
import math

import jax
import jax.numpy as jnp
import numpy as np
from jax import lax
from jax.experimental import pallas as pl
from jax.experimental.pallas import tpu as pltpu
from jax.sharding import Mesh
from jax.sharding import PartitionSpec as P

CH = 128
NT = 512
BIN0 = 8
NOFF = 9
PIECES = (0, 1, 5, 9)


def grant(mib):
    return pltpu.CompilerParams(vmem_limit_bytes=mib * 1024 * 1024)


def slot_bins(bins):
    return lambda slot: bins // 4 * (slot // (bins // 4)) + 2 * (slot % (bins // 8)) + slot // (bins // 8) % 2


def basis_rows(bins):
    t = np.arange(NT)
    kept = BIN0 + slot_bins(bins)(np.arange(bins))
    phase = (t[:, None] * kept[None, :] % NT).astype(np.float32)
    angles = np.float32(2.0 * math.pi / NT) * phase
    taper = np.float32(0.5) - np.float32(0.5) * np.cos(np.float32(2.0 * math.pi / NT) * t.astype(np.float32))
    table = np.concatenate([taper[:, None] * np.cos(angles), -taper[:, None] * np.sin(angles)], axis=1)
    return jnp.asarray(table.T.astype(jnp.bfloat16))


def spectra_body(strain, live, order, basis, whiten, out, held, place, loaded, *, parts):
    windows = strain.shape[0]
    bins = basis.shape[0] // 2
    rows = 2 * windows
    size = windows // parts

    def load(i):
        part = pl.ds(i * size, size)
        return pltpu.make_async_copy(strain.at[part], held.at[part], loaded.at[i])

    for i in range(parts):
        load(i).start()
    channel = lax.broadcasted_iota(jnp.int32, (CH, CH), 0)
    pick = (channel == order[...]).astype(jnp.float32).astype(jnp.bfloat16)
    row = lax.broadcasted_iota(jnp.int32, (2 * bins, bins), 0)
    column = lax.broadcasted_iota(jnp.int32, (2 * bins, bins), 1)
    spread = jnp.where(column == slot_bins(bins)(row % bins), whiten[...], 0.0)
    gain = jnp.sum(spread, axis=1, keepdims=True) * (2.0 / math.sqrt(NT))
    for i in range(parts):
        load(i).wait()
        for at in range(i * size, (i + 1) * size):
            value = held[at].astype(jnp.float32)
            centered = value - jnp.sum(value, axis=1, keepdims=True) * (1.0 / NT)
            power = jnp.sum(centered * centered, axis=1, keepdims=True) * (1.0 / NT)
            normed = (centered * lax.rsqrt(power + 1e-06)).astype(jnp.bfloat16)
            spec = lax.dot_general(basis[...], normed, (((1,), (1,)), ((), ())), preferred_element_type=jnp.float32)
            weight = live[at : at + 1, :].astype(jnp.float32)
            spec = (spec * gain * weight).astype(jnp.bfloat16)
            spec = jnp.dot(spec, pick, preferred_element_type=jnp.float32)
            for s in range(2):
                place[pl.ds(2 * at + s, bins, stride=rows), :] = spec[s * bins : (s + 1) * bins]
    for x in range(4):
        part = slice(x * bins * rows // 4, (x + 1) * bins * rows // 4)
        out[part] = place[part].astype(jnp.bfloat16)


def spectra(strain, live, order, basis, whiten):
    windows = strain.shape[0]
    total = basis.shape[0] * windows
    parts = 4 if windows % 4 == 0 else 1
    whole = pl.BlockSpec(memory_space=pltpu.VMEM)
    return pl.pallas_call(
        functools.partial(spectra_body, parts=parts),
        in_specs=[pl.BlockSpec(memory_space=pl.ANY)] + [whole] * 4,
        out_specs=whole,
        out_shape=jax.ShapeDtypeStruct((total, CH), jnp.bfloat16),
        scratch_shapes=[
            pltpu.VMEM((windows, CH, NT), jnp.bfloat16),
            pltpu.VMEM((total, CH), jnp.float32),
            pltpu.SemaphoreType.DMA((parts,)),
        ],
        name="spectra",
    )(strain, live, order, basis, whiten)


def left_body(where, data, left, piece, *, scale):
    half = where[0]
    for i, side in enumerate((half, 1 - half)):
        block = data[:, side].reshape(-1, CH)
        own = block.astype(jnp.float32).reshape(-1, 8, CH)
        part = lax.broadcasted_iota(jnp.int32, own.shape, 1)
        turned = jnp.where(part % 2 == 0, pltpu.roll(own, 7, 1), -pltpu.roll(own, 1, 1))
        own = own.reshape(-1, CH).T.astype(jnp.bfloat16)
        turned = turned.reshape(-1, CH).T.astype(jnp.bfloat16)
        left[(2 * i) * CH : (2 * i + 1) * CH] = own
        left[(2 * i + 1) * CH : (2 * i + 2) * CH] = turned
        if i == 1:
            for s, value in enumerate((own, turned)):
                total = jnp.dot(value, block, preferred_element_type=jnp.float32)
                piece[0, s] = (total * scale).astype(jnp.bfloat16)


def left_of(where, data, scale):
    whole = pl.BlockSpec(memory_space=pltpu.VMEM)
    return pl.pallas_call(
        functools.partial(left_body, scale=scale),
        in_specs=[pl.BlockSpec(memory_space=pltpu.SMEM), whole],
        out_specs=[whole, whole],
        out_shape=[
            jax.ShapeDtypeStruct((4 * CH, data.shape[0] * data.shape[2]), jnp.bfloat16),
            jax.ShapeDtypeStruct((1, 2, CH, CH), jnp.bfloat16),
        ],
        compiler_params=grant(12),
        name="left",
    )(where, data)


def product_body(where, left, *refs, aheads, scale, begun):
    count = 2 * len(aheads)
    data = refs[:count]
    outs = refs[count + begun :]
    if begun == 2:
        out, later, kept, sent, kept_done, sent_done = outs
        now = None
    else:
        out, now, later, kept, sent, kept_done, sent_done = outs
    half, core = where[0], where[1]
    jobs = []
    for i, ahead in enumerate(aheads):
        for other in range(2):
            ref = data[2 * i + other]
            right = jnp.concatenate([ref[:, 0].reshape(-1, CH), ref[:, 1].reshape(-1, CH)], axis=1)
            total = jnp.dot(left[...], right, preferred_element_type=jnp.float32) * scale
            for side in range(2):
                spot = (2 * i + other) * 2 + side
                columns = slice(side * CH, (side + 1) * CH)
                turn = 4 * ahead + other * (1 - 2 * core)
                for s in range(2):
                    kept[spot, s] = total[s * CH : (s + 1) * CH, columns]
                    sent[spot, s] = total[(2 + s) * CH : (3 + s) * CH, columns].astype(jnp.bfloat16)
                offset = turn + 2 * (side - half)
                target = jnp.clip(offset, 0, NOFF - 1)
                copy = pltpu.make_async_copy(kept.at[spot], out.at[half, :, target], kept_done.at[spot])
                jobs.append((jnp.logical_and(offset >= 0, offset < NOFF), copy))
                offset = turn + 2 * (side - 1 + half)
                target = jnp.clip(offset - PIECES[2], 0, PIECES[3] - PIECES[2] - 1)
                copy = pltpu.make_async_copy(sent.at[spot], later.at[target], sent_done.at[spot])
                jobs.append((jnp.logical_and(offset >= PIECES[2], offset < PIECES[3]), copy))
                if now is not None:
                    target = jnp.clip(offset - PIECES[1], 0, PIECES[2] - PIECES[1] - 1)
                    copy = pltpu.make_async_copy(sent.at[spot], now.at[target], sent_done.at[spot])
                    jobs.append((jnp.logical_and(offset >= PIECES[1], offset < PIECES[2]), copy))
                for valid, copy in jobs[-3 if now is not None else -2 :]:
                    pl.when(valid)(copy.start)
    for valid, copy in jobs:
        pl.when(valid)(copy.wait)


def products(where, left, data, begun, aheads, scale):
    whole = pl.BlockSpec(memory_space=pltpu.VMEM)
    somewhere = pl.BlockSpec(memory_space=pl.ANY)
    spots = 4 * len(aheads)
    out = jax.ShapeDtypeStruct((2, 2, NOFF, CH, CH), jnp.float32)
    piece = [jax.ShapeDtypeStruct((PIECES[i + 1] - PIECES[i], 2, CH, CH), jnp.bfloat16) for i in (1, 2)]
    outs = [out, piece[1]] if begun else [out, *piece]
    first = 2 + len(data)
    return pl.pallas_call(
        functools.partial(product_body, aheads=aheads, scale=scale, begun=len(begun)),
        in_specs=[pl.BlockSpec(memory_space=pltpu.SMEM)] + [whole] * (1 + len(data)) + [somewhere] * len(begun),
        out_specs=[somewhere] * len(outs),
        out_shape=outs,
        input_output_aliases={first + i: i for i in range(len(begun))},
        scratch_shapes=[
            pltpu.VMEM((spots, 2, CH, CH), jnp.float32),
            pltpu.VMEM((spots, 2, CH, CH), jnp.bfloat16),
            pltpu.SemaphoreType.DMA((spots,)),
            pltpu.SemaphoreType.DMA((spots,)),
        ],
        compiler_params=grant(20),
        name="products",
    )(where, left, *data, *begun)


def merge_body(where, piece, filled, out, stage, done, *, first):
    copies = []
    for i in range(piece.shape[0]):
        stage[i] = piece[i].astype(jnp.float32)
        copies.append(pltpu.make_async_copy(stage.at[i], out.at[1 - where[0], :, first + i], done.at[i]))
        copies[-1].start()
    for copy in copies:
        copy.wait()


def merged(where, piece, filled, first):
    whole = pl.BlockSpec(memory_space=pltpu.VMEM)
    somewhere = pl.BlockSpec(memory_space=pl.ANY)
    return pl.pallas_call(
        functools.partial(merge_body, first=first),
        in_specs=[pl.BlockSpec(memory_space=pltpu.SMEM), whole, somewhere],
        out_specs=somewhere,
        out_shape=jax.ShapeDtypeStruct(filled.shape, filled.dtype),
        input_output_aliases={2: 0},
        scratch_shapes=[pltpu.VMEM(piece.shape, jnp.float32), pltpu.SemaphoreType.DMA((piece.shape[0],))],
        compiler_params=grant(8),
        name="merge",
    )(where, piece, filled)


def shifted(value, axis, steps):
    count = lax.axis_size(axis)
    return lax.ppermute(value, axis, [(s, (s + steps) % count) for s in range(count)])


def local(strain, fiber_order, window_valid, whiten):
    bins = whiten.shape[0]
    windows = strain.shape[1]
    strain = jnp.transpose(strain, (1, 0, 2))
    live = jnp.transpose(window_valid)
    where = jnp.stack([lax.axis_index("z_hi"), lax.axis_index("core")]).astype(jnp.int32)
    scale = 1.0 / math.sqrt(windows * lax.axis_size("x") * lax.axis_size("z_lo"))
    sent = spectra(strain, live, fiber_order, basis_rows(bins), whiten.reshape(1, -1))
    here = lax.all_to_all(sent.reshape(bins, 2 * windows, CH), ("x", "z_hi", "z_lo"), 0, 0, tiled=True)
    here = here.reshape(4, 2, -1, CH)
    ahead1 = shifted(here, "y", -1)
    ahead2 = shifted(here, "y", 1)
    other0 = shifted(here, "core", 1)
    left, piece0 = left_of(where, here, scale)
    ahead1, left, piece0 = lax.optimization_barrier((ahead1, left, piece0))
    piece0 = shifted(piece0, "z_hi", 1)
    ahead2 = shifted(ahead2, "y", 1)
    other1 = shifted(ahead1, "core", 1)
    left, piece0 = lax.optimization_barrier((left, piece0))
    out, piece1, piece2 = products(where, left, [here, other0, ahead1, other1], [], (0, 1), scale)
    ahead2, out, piece2 = lax.optimization_barrier((ahead2, out, piece2))
    piece1 = shifted(piece1, "z_hi", 1)
    other2 = shifted(ahead2, "core", 1)
    out, piece2 = products(where, left, [ahead2, other2], [out, piece2], (2,), scale)
    piece2 = shifted(piece2, "z_hi", 1)
    for first, piece in zip(PIECES, (piece0, piece1, piece2)):
        out = merged(where, piece, out, first)
    return out


def solution(mesh):
    fine = Mesh(mesh.devices.reshape(4, 8, 4, 2, 2), ("x", "z_lo", "y", "z_hi", "core"))
    freq, chan = ("x", "z_lo"), ("y", "z_hi", "core")
    in_specs = (P(chan, freq, None), P(chan, None), P(chan, freq), P())
    out_specs = P(freq, None, None, chan, None)
    return jax.shard_map(local, mesh=fine, in_specs=in_specs, out_specs=out_specs, check_vma=False)
```

```python
import functools
import math

import jax
import jax.numpy as jnp
import numpy as np
from jax import lax
from jax.experimental import pallas as pl
from jax.experimental.pallas import tpu as pltpu
from jax.sharding import Mesh
from jax.sharding import PartitionSpec as P

CH = 128
NT = 512
BIN0 = 8
GROUP = 4
CHUNKS = (12, 8)
NOFF = 9


def grant(mib):
    return pltpu.CompilerParams(vmem_limit_bytes=mib * 1024 * 1024)


def basis_rows(groups):
    t = np.arange(NT)
    bins = BIN0 + np.arange(2 * groups)
    phase = (t[:, None] * bins[None, :] % NT).astype(np.float32)
    angles = np.float32(2.0 * math.pi / NT) * phase
    taper = np.float32(0.5) - np.float32(0.5) * np.cos(np.float32(2.0 * math.pi / NT) * t.astype(np.float32))
    table = np.stack([taper[:, None] * np.cos(angles), -taper[:, None] * np.sin(angles)], axis=2)
    table = table.reshape(NT, groups, 4).transpose(2, 1, 0).reshape(4 * groups, NT)
    return jnp.asarray(table.astype(jnp.bfloat16))


def spectra_body(strain, live, order, basis, whiten, out, held, place, loaded, *, first, count, groups):
    rows = 4 * count

    def load(i):
        part = pl.ds(first + i * GROUP, GROUP)
        return pltpu.make_async_copy(strain.at[part], held.at[pl.ds(i * GROUP, GROUP)], loaded.at[i])

    for i in range(count // GROUP):
        load(i).start()
    channel = lax.broadcasted_iota(jnp.int32, (CH, CH), 0)
    pick = (channel == order[...]).astype(jnp.float32).astype(jnp.bfloat16)
    shape = (4 * groups, 2 * groups)
    row = lax.broadcasted_iota(jnp.int32, shape, 0)
    column = lax.broadcasted_iota(jnp.int32, shape, 1)
    spread = jnp.where(column == 2 * (row % groups) + row // (2 * groups), whiten[...], 0.0)
    gain = jnp.sum(spread, axis=1, keepdims=True) * (2.0 / math.sqrt(NT))
    for i in range(count // GROUP):
        load(i).wait()
        for at in range(i * GROUP, (i + 1) * GROUP):
            value = held[at].astype(jnp.float32)
            centered = value - jnp.sum(value, axis=1, keepdims=True) * (1.0 / NT)
            power = jnp.sum(centered * centered, axis=1, keepdims=True) * (1.0 / NT)
            normed = (centered * lax.rsqrt(power + 1e-06)).astype(jnp.bfloat16)
            spec = lax.dot_general(basis[...], normed, (((1,), (1,)), ((), ())), preferred_element_type=jnp.float32)
            weight = live[first + at : first + at + 1, :].astype(jnp.float32)
            spec = (spec * gain * weight).astype(jnp.bfloat16)
            spec = jnp.dot(spec, pick, preferred_element_type=jnp.float32)
            for part in range(4):
                place[pl.ds(at * 4 + part, groups, stride=rows), :] = spec[part * groups : (part + 1) * groups]
    for x in range(4):
        size = groups * rows // 4
        packed = place[x * size : (x + 1) * size].astype(jnp.bfloat16)
        out[x, 0] = packed
        out[x, 1] = packed


def spectra(strain, live, order, basis, whiten, first, count):
    groups = basis.shape[0] // 4
    rows = 4 * count
    whole = pl.BlockSpec(memory_space=pltpu.VMEM)
    return pl.pallas_call(
        functools.partial(spectra_body, first=first, count=count, groups=groups),
        in_specs=[pl.BlockSpec(memory_space=pl.ANY)] + [whole] * 4,
        out_specs=whole,
        out_shape=jax.ShapeDtypeStruct((4, 2, groups * rows // 4, CH), jnp.bfloat16),
        scratch_shapes=[
            pltpu.VMEM((count, CH, NT), jnp.bfloat16),
            pltpu.VMEM((groups * rows, CH), jnp.float32),
            pltpu.SemaphoreType.DMA((count // GROUP,)),
        ],
        name="spectra",
    )(strain, live, order, basis, whiten)


def left_body(where, data, out):
    own = data[:, where[0]]
    own = own.reshape(-1, CH).astype(jnp.float32)
    own = own.reshape(-1, 8, CH)
    part = lax.broadcasted_iota(jnp.int32, own.shape, 1)
    turned = jnp.where(part % 2 == 0, pltpu.roll(own, 7, 1), -pltpu.roll(own, 1, 1))
    own = own.reshape(-1, CH).T
    turned = turned.reshape(-1, CH).T
    first = lax.broadcasted_iota(jnp.int32, own.shape, 1) % 4 < 2
    zero = jnp.zeros_like(own)
    out[0 * CH : 1 * CH] = jnp.where(first, own, zero).astype(jnp.bfloat16)
    out[1 * CH : 2 * CH] = jnp.where(first, turned, zero).astype(jnp.bfloat16)
    out[2 * CH : 3 * CH] = jnp.where(first, zero, own).astype(jnp.bfloat16)
    out[3 * CH : 4 * CH] = jnp.where(first, zero, turned).astype(jnp.bfloat16)


def left_of(where, data):
    whole = pl.BlockSpec(memory_space=pltpu.VMEM)
    return pl.pallas_call(
        left_body,
        in_specs=[pl.BlockSpec(memory_space=pltpu.SMEM), whole],
        out_specs=whole,
        out_shape=jax.ShapeDtypeStruct((4 * CH, data.shape[0] * data.shape[2]), jnp.bfloat16),
        compiler_params=grant(12),
        name="left",
    )(where, data)


def product(left, ref):
    right = jnp.concatenate([ref[:, 0].reshape(-1, CH), ref[:, 1].reshape(-1, CH)], axis=1)
    return jnp.dot(left[...], right, preferred_element_type=jnp.float32)


def early_body(left, *refs):
    for i in range(6):
        refs[6 + i // 2][i % 2] = product(left, refs[i])


def early(left, data):
    whole = pl.BlockSpec(memory_space=pltpu.VMEM)
    return pl.pallas_call(
        early_body,
        in_specs=[whole] * 7,
        out_specs=[whole] * 3,
        out_shape=[jax.ShapeDtypeStruct((2, 4 * CH, 2 * CH), jnp.float32)] * 3,
        cost_estimate=pl.CostEstimate(flops=7 * 10**9, transcendentals=0, bytes_accessed=12 * 10**6),
        compiler_params=grant(24),
        name="early",
    )(left, *data)


def late_body(where, left, begun, one, two, *refs, ahead, scale):
    out, stage, done = refs[-3:]
    half, core = where[0], where[1]
    jobs = []
    for other, ref in enumerate((one, two)):
        total = (begun[other] + product(left, ref)) * scale
        for side in range(2):
            spot = 2 * other + side
            for part in range(4):
                row = part * CH
                stage[spot, part // 2, part % 2] = total[row : row + CH, side * CH : (side + 1) * CH]
            offset = 4 * ahead + 2 * (side - half) + other * (1 - 2 * core)
            valid = jnp.logical_and(offset >= 0, offset < NOFF)
            target = jnp.clip(offset, 0, NOFF - 1)
            copy = pltpu.make_async_copy(stage.at[spot], out.at[:, :, target], done.at[spot])
            jobs.append((valid, copy))
            pl.when(valid)(copy.start)
    for valid, copy in jobs:
        pl.when(valid)(copy.wait)


def late(where, left, begun, one, two, filled, ahead, scale):
    whole = pl.BlockSpec(memory_space=pltpu.VMEM)
    somewhere = pl.BlockSpec(memory_space=pl.ANY)
    extra = [] if filled is None else [filled]
    return pl.pallas_call(
        functools.partial(late_body, ahead=ahead, scale=scale),
        in_specs=[
            pl.BlockSpec(memory_space=pltpu.SMEM),
            whole,
            whole,
            whole,
            whole,
        ]
        + [somewhere] * len(extra),
        out_specs=somewhere,
        out_shape=jax.ShapeDtypeStruct((2, 2, NOFF, CH, CH), jnp.float32),
        input_output_aliases={5: 0} if extra else {},
        scratch_shapes=[pltpu.VMEM((4, 2, 2, CH, CH), jnp.float32), pltpu.SemaphoreType.DMA((4,))],
        cost_estimate=pl.CostEstimate(flops=2 * 10**9, transcendentals=0, bytes_accessed=4 * 10**6),
        compiler_params=grant(16),
        name="late",
    )(where, left, begun, one, two, *extra)


def shifted(value, axis, steps):
    count = lax.axis_size(axis)
    return lax.ppermute(value, axis, [(s, (s + steps) % count) for s in range(count)])


def upper(value, steps):
    count = lax.axis_size("y")
    pairs = [(2 * y + 1, 2 * ((y + steps) % count) + 1) for y in range(count)]
    return lax.ppermute(value, ("y", "z_hi"), pairs)


def fetched(here, direct):
    ahead1 = shifted(here, "y", -1)
    if direct:
        low = shifted(here[:, 0], "y", 2)
    else:
        low = shifted(shifted(here[:, 0], "y", 1), "y", 1)
    return [here, ahead1, jnp.stack([low, upper(here[:, 1], 2)], axis=1)]


def both(own):
    return [w for v in own for w in (v, shifted(v, "core", 1))]


def local(strain, fiber_order, window_valid, whiten):
    groups = whiten.shape[0] // 2
    windows = strain.shape[1]
    strain = jnp.transpose(strain, (1, 0, 2))
    live = jnp.transpose(window_valid)
    basis = basis_rows(groups)
    where = jnp.stack([lax.axis_index("z_hi"), lax.axis_index("core")]).astype(jnp.int32)
    scale = 1.0 / math.sqrt(windows * lax.axis_size("x") * lax.axis_size("z_lo"))

    def made(first, count):
        sent = spectra(strain, live, fiber_order, basis, whiten.reshape(1, -1), first, count)
        return sent.reshape(2 * groups, 4 * count, CH)

    def spread(sent):
        here = lax.all_to_all(sent, ("x", "z_hi", "z_lo"), 0, 0, tiled=True)
        return here.reshape(4, 2, -1, CH)

    first, second = spread(made(0, CHUNKS[0])), made(*CHUNKS)
    first, second = lax.optimization_barrier((first, second))
    head = both(fetched(first, False))
    tail = spread(second)
    tail, *head = lax.optimization_barrier((tail, *head))
    rest = fetched(tail, True)
    begun = early(left_of(where, head[0]), head)
    left = left_of(where, tail)
    ahead1, ahead2, left, *begun = lax.optimization_barrier((*rest[1:], left, *begun))
    data = both([tail, ahead1, ahead2])
    filled = None
    for ahead in range(3):
        one, two = data[2 * ahead : 2 * ahead + 2]
        filled = late(where, left, begun[ahead], one, two, filled, ahead, scale)
    return filled


def solution(mesh):
    fine = Mesh(mesh.devices.reshape(4, 8, 4, 2, 2), ("x", "z_lo", "y", "z_hi", "core"))
    freq, chan = ("x", "z_lo"), ("y", "z_hi", "core")
    in_specs = (P(chan, freq, None), P(chan, None), P(chan, freq), P())
    out_specs = P(freq, None, None, chan, None)
    return jax.shard_map(local, mesh=fine, in_specs=in_specs, out_specs=out_specs, check_vma=False)
```

```python
import functools
import math

import jax
import jax.numpy as jnp
import numpy as np
from jax import lax
from jax.experimental import pallas as pl
from jax.experimental.pallas import tpu as pltpu
from jax.sharding import Mesh
from jax.sharding import PartitionSpec as P

CH = 128
NT = 512
BIN0 = 8
GROUP = 5
CHUNKS = (10, 10)
NOFF = 9


def grant(mib):
    return pltpu.CompilerParams(vmem_limit_bytes=mib * 1024 * 1024)


def basis_rows(groups):
    t = np.arange(NT)
    bins = BIN0 + np.arange(2 * groups)
    phase = (t[:, None] * bins[None, :] % NT).astype(np.float32)
    angles = np.float32(2.0 * math.pi / NT) * phase
    taper = np.float32(0.5) - np.float32(0.5) * np.cos(np.float32(2.0 * math.pi / NT) * t.astype(np.float32))
    table = np.stack([taper[:, None] * np.cos(angles), -taper[:, None] * np.sin(angles)], axis=2)
    table = table.reshape(NT, groups, 4).transpose(2, 1, 0).reshape(4 * groups, NT)
    return jnp.asarray(table.astype(jnp.bfloat16))


def spectra_body(strain, live, order, basis, whiten, out, held, place, loaded, *, first, count, groups):
    rows = 4 * count

    def load(i):
        part = pl.ds(first + i * GROUP, GROUP)
        return pltpu.make_async_copy(strain.at[part], held.at[pl.ds(i * GROUP, GROUP)], loaded.at[i])

    for i in range(count // GROUP):
        load(i).start()
    channel = lax.broadcasted_iota(jnp.int32, (CH, CH), 0)
    pick = (channel == order[...]).astype(jnp.float32).astype(jnp.bfloat16)
    shape = (4 * groups, 2 * groups)
    row = lax.broadcasted_iota(jnp.int32, shape, 0)
    column = lax.broadcasted_iota(jnp.int32, shape, 1)
    spread = jnp.where(column == 2 * (row % groups) + row // (2 * groups), whiten[...], 0.0)
    gain = jnp.sum(spread, axis=1, keepdims=True) * (2.0 / math.sqrt(NT))
    for i in range(count // GROUP):
        load(i).wait()
        for at in range(i * GROUP, (i + 1) * GROUP):
            value = held[at].astype(jnp.float32)
            centered = value - jnp.sum(value, axis=1, keepdims=True) * (1.0 / NT)
            power = jnp.sum(centered * centered, axis=1, keepdims=True) * (1.0 / NT)
            normed = (centered * lax.rsqrt(power + 1e-06)).astype(jnp.bfloat16)
            spec = lax.dot_general(basis[...], normed, (((1,), (1,)), ((), ())), preferred_element_type=jnp.float32)
            weight = live[first + at : first + at + 1, :].astype(jnp.float32)
            spec = (spec * gain * weight).astype(jnp.bfloat16)
            spec = jnp.dot(spec, pick, preferred_element_type=jnp.float32)
            for part in range(4):
                place[pl.ds(at * 4 + part, groups, stride=rows), :] = spec[part * groups : (part + 1) * groups]
    for x in range(4):
        size = groups * rows // 4
        packed = place[x * size : (x + 1) * size].astype(jnp.bfloat16)
        out[x, 0] = packed
        out[x, 1] = packed


def spectra(strain, live, order, basis, whiten, first, count):
    groups = basis.shape[0] // 4
    rows = 4 * count
    whole = pl.BlockSpec(memory_space=pltpu.VMEM)
    return pl.pallas_call(
        functools.partial(spectra_body, first=first, count=count, groups=groups),
        in_specs=[pl.BlockSpec(memory_space=pl.ANY)] + [whole] * 4,
        out_specs=whole,
        out_shape=jax.ShapeDtypeStruct((4, 2, groups * rows // 4, CH), jnp.bfloat16),
        scratch_shapes=[
            pltpu.VMEM((count, CH, NT), jnp.bfloat16),
            pltpu.VMEM((groups * rows, CH), jnp.float32),
            pltpu.SemaphoreType.DMA((count // GROUP,)),
        ],
        name="spectra",
    )(strain, live, order, basis, whiten)


def left_body(where, data, out):
    own = data[:, where[0]]
    own = own.reshape(-1, CH).astype(jnp.float32)
    own = own.reshape(-1, 8, CH)
    part = lax.broadcasted_iota(jnp.int32, own.shape, 1)
    turned = jnp.where(part % 2 == 0, pltpu.roll(own, 7, 1), -pltpu.roll(own, 1, 1))
    own = own.reshape(-1, CH).T
    turned = turned.reshape(-1, CH).T
    first = lax.broadcasted_iota(jnp.int32, own.shape, 1) % 4 < 2
    zero = jnp.zeros_like(own)
    out[0 * CH : 1 * CH] = jnp.where(first, own, zero).astype(jnp.bfloat16)
    out[1 * CH : 2 * CH] = jnp.where(first, turned, zero).astype(jnp.bfloat16)
    out[2 * CH : 3 * CH] = jnp.where(first, zero, own).astype(jnp.bfloat16)
    out[3 * CH : 4 * CH] = jnp.where(first, zero, turned).astype(jnp.bfloat16)


def left_of(where, data):
    whole = pl.BlockSpec(memory_space=pltpu.VMEM)
    return pl.pallas_call(
        left_body,
        in_specs=[pl.BlockSpec(memory_space=pltpu.SMEM), whole],
        out_specs=whole,
        out_shape=jax.ShapeDtypeStruct((4 * CH, data.shape[0] * data.shape[2]), jnp.bfloat16),
        compiler_params=grant(12),
        name="left",
    )(where, data)


def product(left, ref):
    right = jnp.concatenate([ref[:, 0].reshape(-1, CH), ref[:, 1].reshape(-1, CH)], axis=1)
    return jnp.dot(left[...], right, preferred_element_type=jnp.float32)


def early_body(left, *refs):
    for i in range(6):
        refs[6 + i // 2][i % 2] = product(left, refs[i])


def early(left, data):
    whole = pl.BlockSpec(memory_space=pltpu.VMEM)
    return pl.pallas_call(
        early_body,
        in_specs=[whole] * 7,
        out_specs=[whole] * 3,
        out_shape=[jax.ShapeDtypeStruct((2, 4 * CH, 2 * CH), jnp.float32)] * 3,
        cost_estimate=pl.CostEstimate(flops=7 * 10**9, transcendentals=0, bytes_accessed=12 * 10**6),
        compiler_params=grant(24),
        name="early",
    )(left, *data)


def late_body(where, left, begun, one, two, *refs, ahead, scale):
    out, stage, done = refs[-3:]
    half, core = where[0], where[1]
    jobs = []
    for other, ref in enumerate((one, two)):
        total = (begun[other] + product(left, ref)) * scale
        for side in range(2):
            spot = 2 * other + side
            for part in range(4):
                row = part * CH
                stage[spot, part // 2, part % 2] = total[row : row + CH, side * CH : (side + 1) * CH]
            offset = 4 * ahead + 2 * (side - half) + other * (1 - 2 * core)
            valid = jnp.logical_and(offset >= 0, offset < NOFF)
            target = jnp.clip(offset, 0, NOFF - 1)
            copy = pltpu.make_async_copy(stage.at[spot], out.at[:, :, target], done.at[spot])
            jobs.append((valid, copy))
            pl.when(valid)(copy.start)
    for valid, copy in jobs:
        pl.when(valid)(copy.wait)


def late(where, left, begun, one, two, filled, ahead, scale):
    whole = pl.BlockSpec(memory_space=pltpu.VMEM)
    somewhere = pl.BlockSpec(memory_space=pl.ANY)
    extra = [] if filled is None else [filled]
    return pl.pallas_call(
        functools.partial(late_body, ahead=ahead, scale=scale),
        in_specs=[
            pl.BlockSpec(memory_space=pltpu.SMEM),
            whole,
            whole,
            whole,
            whole,
        ]
        + [somewhere] * len(extra),
        out_specs=somewhere,
        out_shape=jax.ShapeDtypeStruct((2, 2, NOFF, CH, CH), jnp.float32),
        input_output_aliases={5: 0} if extra else {},
        scratch_shapes=[pltpu.VMEM((4, 2, 2, CH, CH), jnp.float32), pltpu.SemaphoreType.DMA((4,))],
        cost_estimate=pl.CostEstimate(flops=2 * 10**9, transcendentals=0, bytes_accessed=4 * 10**6),
        compiler_params=grant(16),
        name="late",
    )(where, left, begun, one, two, *extra)


def shifted(value, axis, steps):
    count = lax.axis_size(axis)
    return lax.ppermute(value, axis, [(s, (s + steps) % count) for s in range(count)])


def upper(value, steps):
    count = lax.axis_size("y")
    pairs = [(2 * y + 1, 2 * ((y + steps) % count) + 1) for y in range(count)]
    return lax.ppermute(value, ("y", "z_hi"), pairs)


def fetched(here, held):
    ahead1 = shifted(here, "y", -1)
    low, *held = lax.optimization_barrier((shifted(here[:, 0], "y", 1), *held))
    return [here, ahead1, jnp.stack([shifted(low, "y", 1), upper(here[:, 1], 2)], axis=1)], held


def both(own):
    return [w for v in own for w in (v, shifted(v, "core", 1))]


def local(strain, fiber_order, window_valid, whiten):
    groups = whiten.shape[0] // 2
    windows = strain.shape[1]
    strain = jnp.transpose(strain, (1, 0, 2))
    live = jnp.transpose(window_valid)
    basis = basis_rows(groups)
    where = jnp.stack([lax.axis_index("z_hi"), lax.axis_index("core")]).astype(jnp.int32)
    scale = 1.0 / math.sqrt(windows * lax.axis_size("x") * lax.axis_size("z_lo"))

    def made(first, count):
        sent = spectra(strain, live, fiber_order, basis, whiten.reshape(1, -1), first, count)
        return sent.reshape(2 * groups, 4 * count, CH)

    def spread(sent):
        here = lax.all_to_all(sent, ("x", "z_hi", "z_lo"), 0, 0, tiled=True)
        return here.reshape(4, 2, -1, CH)

    first, second = spread(made(0, CHUNKS[0])), made(*CHUNKS)
    first, second = lax.optimization_barrier((first, second))
    head = both(fetched(first, [])[0])
    tail = spread(second)
    tail, *head = lax.optimization_barrier((tail, *head))
    (_, ahead1, ahead2), head = fetched(tail, head)
    begun = early(left_of(where, head[0]), head)
    left = left_of(where, tail)
    filled = late(where, left, begun[0], tail, shifted(tail, "core", 1), None, 0, scale)
    ahead1, ahead2, left, filled, *begun = lax.optimization_barrier((ahead1, ahead2, left, filled, *begun))
    data = both([ahead1, ahead2])
    for ahead in (1, 2):
        one, two = data[2 * ahead - 2 : 2 * ahead]
        filled = late(where, left, begun[ahead], one, two, filled, ahead, scale)
    return filled


def solution(mesh):
    fine = Mesh(mesh.devices.reshape(4, 8, 4, 2, 2), ("x", "z_lo", "y", "z_hi", "core"))
    freq, chan = ("x", "z_lo"), ("y", "z_hi", "core")
    in_specs = (P(chan, freq, None), P(chan, None), P(chan, freq), P())
    out_specs = P(freq, None, None, chan, None)
    return jax.shard_map(local, mesh=fine, in_specs=in_specs, out_specs=out_specs, check_vma=False)
```

```python
import functools
import math

import jax
import jax.numpy as jnp
import numpy as np
from jax import lax
from jax.experimental import pallas as pl
from jax.experimental.pallas import tpu as pltpu
from jax.sharding import Mesh
from jax.sharding import PartitionSpec as P

CH = 128
NT = 512
BIN0 = 8
GROUP = 5
CHUNKS = (10, 10)
NOFF = 9


def grant(mib):
    return pltpu.CompilerParams(vmem_limit_bytes=mib * 1024 * 1024)


def basis_rows(groups):
    t = np.arange(NT)
    bins = BIN0 + np.arange(2 * groups)
    phase = (t[:, None] * bins[None, :] % NT).astype(np.float32)
    angles = np.float32(2.0 * math.pi / NT) * phase
    taper = np.float32(0.5) - np.float32(0.5) * np.cos(np.float32(2.0 * math.pi / NT) * t.astype(np.float32))
    table = np.stack([taper[:, None] * np.cos(angles), -taper[:, None] * np.sin(angles)], axis=2)
    table = table.reshape(NT, groups, 4).transpose(2, 1, 0).reshape(4 * groups, NT)
    return jnp.asarray(table.astype(jnp.bfloat16))


def spectra_body(strain, live, order, basis, whiten, out, held, place, loaded, *, first, count, groups):
    rows = 4 * count

    def load(i):
        part = pl.ds(first + i * GROUP, GROUP)
        return pltpu.make_async_copy(strain.at[part], held.at[pl.ds(i * GROUP, GROUP)], loaded.at[i])

    for i in range(count // GROUP):
        load(i).start()
    channel = lax.broadcasted_iota(jnp.int32, (CH, CH), 0)
    pick = (channel == order[...]).astype(jnp.float32).astype(jnp.bfloat16)
    shape = (4 * groups, 2 * groups)
    row = lax.broadcasted_iota(jnp.int32, shape, 0)
    column = lax.broadcasted_iota(jnp.int32, shape, 1)
    spread = jnp.where(column == 2 * (row % groups) + row // (2 * groups), whiten[...], 0.0)
    gain = jnp.sum(spread, axis=1, keepdims=True) * (2.0 / math.sqrt(NT))
    for i in range(count // GROUP):
        load(i).wait()
        for at in range(i * GROUP, (i + 1) * GROUP):
            value = held[at].astype(jnp.float32)
            centered = value - jnp.sum(value, axis=1, keepdims=True) * (1.0 / NT)
            power = jnp.sum(centered * centered, axis=1, keepdims=True) * (1.0 / NT)
            normed = (centered * lax.rsqrt(power + 1e-06)).astype(jnp.bfloat16)
            spec = lax.dot_general(basis[...], normed, (((1,), (1,)), ((), ())), preferred_element_type=jnp.float32)
            weight = live[first + at : first + at + 1, :].astype(jnp.float32)
            spec = (spec * gain * weight).astype(jnp.bfloat16)
            spec = jnp.dot(spec, pick, preferred_element_type=jnp.float32)
            for part in range(4):
                place[pl.ds(at * 4 + part, groups, stride=rows), :] = spec[part * groups : (part + 1) * groups]
    for x in range(4):
        size = groups * rows // 4
        packed = place[x * size : (x + 1) * size].astype(jnp.bfloat16)
        out[x, 0] = packed
        out[x, 1] = packed


def spectra(strain, live, order, basis, whiten, first, count):
    groups = basis.shape[0] // 4
    rows = 4 * count
    whole = pl.BlockSpec(memory_space=pltpu.VMEM)
    return pl.pallas_call(
        functools.partial(spectra_body, first=first, count=count, groups=groups),
        in_specs=[pl.BlockSpec(memory_space=pl.ANY)] + [whole] * 4,
        out_specs=whole,
        out_shape=jax.ShapeDtypeStruct((4, 2, groups * rows // 4, CH), jnp.bfloat16),
        scratch_shapes=[
            pltpu.VMEM((count, CH, NT), jnp.bfloat16),
            pltpu.VMEM((groups * rows, CH), jnp.float32),
            pltpu.SemaphoreType.DMA((count // GROUP,)),
        ],
        name="spectra",
    )(strain, live, order, basis, whiten)


def left_body(where, data, out):
    own = data[:, where[0]]
    own = own.reshape(-1, CH).astype(jnp.float32)
    own = own.reshape(-1, 8, CH)
    part = lax.broadcasted_iota(jnp.int32, own.shape, 1)
    turned = jnp.where(part % 2 == 0, pltpu.roll(own, 7, 1), -pltpu.roll(own, 1, 1))
    own = own.reshape(-1, CH).T
    turned = turned.reshape(-1, CH).T
    first = lax.broadcasted_iota(jnp.int32, own.shape, 1) % 4 < 2
    zero = jnp.zeros_like(own)
    out[0 * CH : 1 * CH] = jnp.where(first, own, zero).astype(jnp.bfloat16)
    out[1 * CH : 2 * CH] = jnp.where(first, turned, zero).astype(jnp.bfloat16)
    out[2 * CH : 3 * CH] = jnp.where(first, zero, own).astype(jnp.bfloat16)
    out[3 * CH : 4 * CH] = jnp.where(first, zero, turned).astype(jnp.bfloat16)


def left_of(where, data):
    whole = pl.BlockSpec(memory_space=pltpu.VMEM)
    return pl.pallas_call(
        left_body,
        in_specs=[pl.BlockSpec(memory_space=pltpu.SMEM), whole],
        out_specs=whole,
        out_shape=jax.ShapeDtypeStruct((4 * CH, data.shape[0] * data.shape[2]), jnp.bfloat16),
        compiler_params=grant(12),
        name="left",
    )(where, data)


def product(left, ref):
    right = jnp.concatenate([ref[:, 0].reshape(-1, CH), ref[:, 1].reshape(-1, CH)], axis=1)
    return jnp.dot(left[...], right, preferred_element_type=jnp.float32)


def early_body(left, *refs):
    for i in range(6):
        refs[6 + i // 2][i % 2] = product(left, refs[i])


def early(left, data):
    whole = pl.BlockSpec(memory_space=pltpu.VMEM)
    return pl.pallas_call(
        early_body,
        in_specs=[whole] * 7,
        out_specs=[whole] * 3,
        out_shape=[jax.ShapeDtypeStruct((2, 4 * CH, 2 * CH), jnp.float32)] * 3,
        cost_estimate=pl.CostEstimate(flops=20 * 10**9, transcendentals=0, bytes_accessed=12 * 10**6),
        compiler_params=grant(24),
        name="early",
    )(left, *data)


def late_body(where, left, begun, one, two, *refs, ahead, scale):
    out, stage, done = refs[-3:]
    half, core = where[0], where[1]
    jobs = []
    for other, ref in enumerate((one, two)):
        total = (begun[other] + product(left, ref)) * scale
        for side in range(2):
            spot = 2 * other + side
            for part in range(4):
                row = part * CH
                stage[spot, part // 2, part % 2] = total[row : row + CH, side * CH : (side + 1) * CH]
            offset = 4 * ahead + 2 * (side - half) + other * (1 - 2 * core)
            valid = jnp.logical_and(offset >= 0, offset < NOFF)
            target = jnp.clip(offset, 0, NOFF - 1)
            copy = pltpu.make_async_copy(stage.at[spot], out.at[:, :, target], done.at[spot])
            jobs.append((valid, copy))
            pl.when(valid)(copy.start)
    for valid, copy in jobs:
        pl.when(valid)(copy.wait)


def late(where, left, begun, one, two, filled, ahead, scale):
    whole = pl.BlockSpec(memory_space=pltpu.VMEM)
    somewhere = pl.BlockSpec(memory_space=pl.ANY)
    extra = [] if filled is None else [filled]
    return pl.pallas_call(
        functools.partial(late_body, ahead=ahead, scale=scale),
        in_specs=[
            pl.BlockSpec(memory_space=pltpu.SMEM),
            whole,
            whole,
            whole,
            whole,
        ]
        + [somewhere] * len(extra),
        out_specs=somewhere,
        out_shape=jax.ShapeDtypeStruct((2, 2, NOFF, CH, CH), jnp.float32),
        input_output_aliases={5: 0} if extra else {},
        scratch_shapes=[pltpu.VMEM((4, 2, 2, CH, CH), jnp.float32), pltpu.SemaphoreType.DMA((4,))],
        cost_estimate=pl.CostEstimate(flops=4 * 10**9, transcendentals=0, bytes_accessed=4 * 10**6),
        compiler_params=grant(16),
        name="late",
    )(where, left, begun, one, two, *extra)


def shifted(value, axis, steps):
    count = lax.axis_size(axis)
    return lax.ppermute(value, axis, [(s, (s + steps) % count) for s in range(count)])


def upper(value, steps):
    count = lax.axis_size("y")
    pairs = [(2 * y + 1, 2 * ((y + steps) % count) + 1) for y in range(count)]
    return lax.ppermute(value, ("y", "z_hi"), pairs)


def fetched(here, held):
    ahead1 = shifted(here, "y", -1)
    high = upper(here[:, 1], 2)
    low, here, *held = lax.optimization_barrier((shifted(here[:, 0], "y", 1), here, *held))
    return [here, ahead1, (shifted(low, "y", 1), high)], held


def both(own):
    return [w for v in own for w in (v, shifted(v, "core", 1))]


def local(strain, fiber_order, window_valid, whiten):
    groups = whiten.shape[0] // 2
    windows = strain.shape[1]
    strain = jnp.transpose(strain, (1, 0, 2))
    live = jnp.transpose(window_valid)
    basis = basis_rows(groups)
    where = jnp.stack([lax.axis_index("z_hi"), lax.axis_index("core")]).astype(jnp.int32)
    scale = 1.0 / math.sqrt(windows * lax.axis_size("x") * lax.axis_size("z_lo"))

    def made(first, count):
        sent = spectra(strain, live, fiber_order, basis, whiten.reshape(1, -1), first, count)
        return sent.reshape(2 * groups, 4 * count, CH)

    def spread(sent):
        here = lax.all_to_all(sent, ("x", "z_hi", "z_lo"), 0, 0, tiled=True)
        return here.reshape(4, 2, -1, CH)

    first, second = spread(made(0, CHUNKS[0])), made(*CHUNKS)
    first, second = lax.optimization_barrier((first, second))
    (first, ahead1, ahead2), _ = fetched(first, [])
    head = both([first, ahead1, jnp.stack(ahead2, axis=1)])
    tail = spread(second)
    tail, *head = lax.optimization_barrier((tail, *head))
    (tail, ahead1, ahead2), head = fetched(tail, head)
    begun = early(left_of(where, head[0]), head)
    left = left_of(where, tail)
    filled = late(where, left, begun[0], tail, shifted(tail, "core", 1), None, 0, scale)
    filled = late(where, left, begun[1], ahead1, shifted(ahead1, "core", 1), filled, 1, scale)
    ahead2, filled = lax.optimization_barrier((ahead2, filled))
    ahead2 = jnp.stack(ahead2, axis=1)
    return late(where, left, begun[2], ahead2, shifted(ahead2, "core", 1), filled, 2, scale)


def solution(mesh):
    fine = Mesh(mesh.devices.reshape(4, 8, 4, 2, 2), ("x", "z_lo", "y", "z_hi", "core"))
    freq, chan = ("x", "z_lo"), ("y", "z_hi", "core")
    in_specs = (P(chan, freq, None), P(chan, None), P(chan, freq), P())
    out_specs = P(freq, None, None, chan, None)
    return jax.shard_map(local, mesh=fine, in_specs=in_specs, out_specs=out_specs, check_vma=False)
```

```python
import functools
import math

import jax
import jax.numpy as jnp
import numpy as np
from jax import lax
from jax.experimental import pallas as pl
from jax.experimental.pallas import tpu as pltpu
from jax.sharding import Mesh
from jax.sharding import PartitionSpec as P

CH = 128
NT = 512
BIN0 = 8
GROUP = 5
CHUNKS = (10, 10)
NOFF = 9


def grant(mib):
    return pltpu.CompilerParams(vmem_limit_bytes=mib * 1024 * 1024)


def basis_rows(groups):
    t = np.arange(NT)
    bins = BIN0 + np.arange(2 * groups)
    phase = (t[:, None] * bins[None, :] % NT).astype(np.float32)
    angles = np.float32(2.0 * math.pi / NT) * phase
    taper = np.float32(0.5) - np.float32(0.5) * np.cos(np.float32(2.0 * math.pi / NT) * t.astype(np.float32))
    table = np.stack([taper[:, None] * np.cos(angles), -taper[:, None] * np.sin(angles)], axis=2)
    table = table.reshape(NT, groups, 4).transpose(2, 1, 0).reshape(4 * groups, NT)
    return jnp.asarray(table.astype(jnp.bfloat16))


def spectra_body(*refs, first, count, groups):
    (strain, *small), out = refs[:5], refs[5]
    held, live, order, basis, whiten, place, packed, loaded, ready, gone = refs[6:]
    rows = 4 * count
    copies = []
    for i in range(count // GROUP):
        part = pl.ds(first + i * GROUP, GROUP)
        copies.append(pltpu.make_async_copy(strain.at[part], held.at[pl.ds(i * GROUP, GROUP)], loaded.at[i]))
    fixed = [
        pltpu.make_async_copy(source, target, ready.at[i])
        for i, (source, target) in enumerate(zip(small, (live, order, basis, whiten)))
    ]
    for copy in [*fixed, *copies]:
        copy.start()
    for copy in fixed:
        copy.wait()
    channel = lax.broadcasted_iota(jnp.int32, (CH, CH), 0)
    pick = (channel == order[...]).astype(jnp.float32).astype(jnp.bfloat16)
    shape = (4 * groups, 2 * groups)
    row = lax.broadcasted_iota(jnp.int32, shape, 0)
    column = lax.broadcasted_iota(jnp.int32, shape, 1)
    spread = jnp.where(column == 2 * (row % groups) + row // (2 * groups), whiten[...], 0.0)
    gain = jnp.sum(spread, axis=1, keepdims=True) * (2.0 / math.sqrt(NT))
    for i in range(count // GROUP):
        copies[i].wait()
        for at in range(i * GROUP, (i + 1) * GROUP):
            value = held[at].astype(jnp.float32)
            centered = value - jnp.sum(value, axis=1, keepdims=True) * (1.0 / NT)
            power = jnp.sum(centered * centered, axis=1, keepdims=True) * (1.0 / NT)
            normed = (centered * lax.rsqrt(power + 1e-06)).astype(jnp.bfloat16)
            spec = lax.dot_general(basis[...], normed, (((1,), (1,)), ((), ())), preferred_element_type=jnp.float32)
            weight = live[first + at : first + at + 1, :].astype(jnp.float32)
            spec = (spec * gain * weight).astype(jnp.bfloat16)
            spec = jnp.dot(spec, pick, preferred_element_type=jnp.float32)
            for part in range(4):
                place[pl.ds(at * 4 + part, groups, stride=rows), :] = spec[part * groups : (part + 1) * groups]
    copies = []
    for x in range(4):
        size = groups * rows // 4
        packed[x] = place[x * size : (x + 1) * size].astype(jnp.bfloat16)
        for half in range(2):
            copies.append(pltpu.make_async_copy(packed.at[x], out.at[x, half], gone.at[x, half]))
            copies[-1].start()
    for copy in copies:
        copy.wait()


def spectra(strain, live, order, basis, whiten, first, count):
    groups = basis.shape[0] // 4
    rows = 4 * count
    somewhere = pl.BlockSpec(memory_space=pl.ANY)
    small = (live, order, basis, whiten)
    return pl.pallas_call(
        functools.partial(spectra_body, first=first, count=count, groups=groups),
        in_specs=[somewhere] * 5,
        out_specs=somewhere,
        out_shape=jax.ShapeDtypeStruct((4, 2, groups * rows // 4, CH), jnp.bfloat16),
        scratch_shapes=[
            pltpu.VMEM((count, CH, NT), jnp.bfloat16),
            *[pltpu.VMEM(v.shape, v.dtype) for v in small],
            pltpu.VMEM((groups * rows, CH), jnp.float32),
            pltpu.VMEM((4, groups * rows // 4, CH), jnp.bfloat16),
            pltpu.SemaphoreType.DMA((count // GROUP,)),
            pltpu.SemaphoreType.DMA((4,)),
            pltpu.SemaphoreType.DMA((4, 2)),
        ],
        name="spectra",
    )(strain, *small)


def left_body(where, data, out):
    own = data[:, where[0]]
    own = own.reshape(-1, CH).astype(jnp.float32)
    own = own.reshape(-1, 8, CH)
    part = lax.broadcasted_iota(jnp.int32, own.shape, 1)
    turned = jnp.where(part % 2 == 0, pltpu.roll(own, 7, 1), -pltpu.roll(own, 1, 1))
    own = own.reshape(-1, CH).T
    turned = turned.reshape(-1, CH).T
    first = lax.broadcasted_iota(jnp.int32, own.shape, 1) % 4 < 2
    zero = jnp.zeros_like(own)
    out[0 * CH : 1 * CH] = jnp.where(first, own, zero).astype(jnp.bfloat16)
    out[1 * CH : 2 * CH] = jnp.where(first, turned, zero).astype(jnp.bfloat16)
    out[2 * CH : 3 * CH] = jnp.where(first, zero, own).astype(jnp.bfloat16)
    out[3 * CH : 4 * CH] = jnp.where(first, zero, turned).astype(jnp.bfloat16)


def left_of(where, data):
    whole = pl.BlockSpec(memory_space=pltpu.VMEM)
    return pl.pallas_call(
        left_body,
        in_specs=[pl.BlockSpec(memory_space=pltpu.SMEM), whole],
        out_specs=whole,
        out_shape=jax.ShapeDtypeStruct((4 * CH, data.shape[0] * data.shape[2]), jnp.bfloat16),
        compiler_params=grant(12),
        name="left",
    )(where, data)


def product(left, ref):
    right = jnp.concatenate([ref[:, 0].reshape(-1, CH), ref[:, 1].reshape(-1, CH)], axis=1)
    return jnp.dot(left[...], right, preferred_element_type=jnp.float32)


def early_body(left, *refs):
    for i in range(6):
        refs[6 + i // 2][i % 2] = product(left, refs[i])


def early(left, data):
    whole = pl.BlockSpec(memory_space=pltpu.VMEM)
    return pl.pallas_call(
        early_body,
        in_specs=[whole] * 7,
        out_specs=[whole] * 3,
        out_shape=[jax.ShapeDtypeStruct((2, 4 * CH, 2 * CH), jnp.float32)] * 3,
        cost_estimate=pl.CostEstimate(flops=20 * 10**9, transcendentals=0, bytes_accessed=12 * 10**6),
        compiler_params=grant(24),
        name="early",
    )(left, *data)


def late_body(where, left, begun, one, two, *refs, ahead, scale):
    out, stage, done = refs[-3:]
    half, core = where[0], where[1]
    jobs = []
    for other, ref in enumerate((one, two)):
        total = (begun[other] + product(left, ref)) * scale
        for side in range(2):
            spot = 2 * other + side
            for part in range(4):
                row = part * CH
                stage[spot, part // 2, part % 2] = total[row : row + CH, side * CH : (side + 1) * CH]
            offset = 4 * ahead + 2 * (side - half) + other * (1 - 2 * core)
            valid = jnp.logical_and(offset >= 0, offset < NOFF)
            target = jnp.clip(offset, 0, NOFF - 1)
            copy = pltpu.make_async_copy(stage.at[spot], out.at[:, :, target], done.at[spot])
            jobs.append((valid, copy))
            pl.when(valid)(copy.start)
    for valid, copy in jobs:
        pl.when(valid)(copy.wait)


def late(where, left, begun, one, two, filled, ahead, scale):
    whole = pl.BlockSpec(memory_space=pltpu.VMEM)
    somewhere = pl.BlockSpec(memory_space=pl.ANY)
    extra = [] if filled is None else [filled]
    return pl.pallas_call(
        functools.partial(late_body, ahead=ahead, scale=scale),
        in_specs=[
            pl.BlockSpec(memory_space=pltpu.SMEM),
            whole,
            whole,
            whole,
            whole,
        ]
        + [somewhere] * len(extra),
        out_specs=somewhere,
        out_shape=jax.ShapeDtypeStruct((2, 2, NOFF, CH, CH), jnp.float32),
        input_output_aliases={5: 0} if extra else {},
        scratch_shapes=[pltpu.VMEM((4, 2, 2, CH, CH), jnp.float32), pltpu.SemaphoreType.DMA((4,))],
        cost_estimate=pl.CostEstimate(flops=4 * 10**9, transcendentals=0, bytes_accessed=4 * 10**6),
        compiler_params=grant(16),
        name="late",
    )(where, left, begun, one, two, *extra)


def shifted(value, axis, steps):
    count = lax.axis_size(axis)
    return lax.ppermute(value, axis, [(s, (s + steps) % count) for s in range(count)])


def upper(value, steps):
    count = lax.axis_size("y")
    pairs = [(2 * y + 1, 2 * ((y + steps) % count) + 1) for y in range(count)]
    return lax.ppermute(value, ("y", "z_hi"), pairs)


def hopped(here):
    low = shifted(shifted(here[:, 0], "y", 1), "y", 1)
    return [here, shifted(here, "y", -1), jnp.stack([low, upper(here[:, 1], 2)], axis=1)]


def both(own):
    return [w for v in own for w in (v, shifted(v, "core", 1))]


def local(strain, fiber_order, window_valid, whiten):
    groups = whiten.shape[0] // 2
    windows = strain.shape[1]
    strain = jnp.transpose(strain, (1, 0, 2))
    live = jnp.transpose(window_valid)
    basis = basis_rows(groups)
    where = jnp.stack([lax.axis_index("z_hi"), lax.axis_index("core")]).astype(jnp.int32)
    scale = 1.0 / math.sqrt(windows * lax.axis_size("x") * lax.axis_size("z_lo"))

    def made(first, count):
        sent = spectra(strain, live, fiber_order, basis, whiten.reshape(1, -1), first, count)
        return sent.reshape(2 * groups, 4 * count, CH)

    def spread(sent):
        here = lax.all_to_all(sent, ("x", "z_hi", "z_lo"), 0, 0, tiled=True)
        return here.reshape(4, 2, -1, CH)

    first, second = spread(made(0, CHUNKS[0])), made(*CHUNKS)
    first, second = lax.optimization_barrier((first, second))
    head = both(hopped(first))
    tail = spread(second)
    tail, *head = lax.optimization_barrier((tail, *head))
    ahead1, ahead2 = shifted(tail, "y", -1), shifted(tail, "y", 2)
    begun = early(left_of(where, head[0]), head)
    left = left_of(where, tail)
    filled = late(where, left, begun[0], tail, shifted(tail, "core", 1), None, 0, scale)
    filled = late(where, left, begun[1], ahead1, shifted(ahead1, "core", 1), filled, 1, scale)
    ahead2, filled = lax.optimization_barrier((ahead2, filled))
    return late(where, left, begun[2], ahead2, shifted(ahead2, "core", 1), filled, 2, scale)


def solution(mesh):
    fine = Mesh(mesh.devices.reshape(4, 8, 4, 2, 2), ("x", "z_lo", "y", "z_hi", "core"))
    freq, chan = ("x", "z_lo"), ("y", "z_hi", "core")
    in_specs = (P(chan, freq, None), P(chan, None), P(chan, freq), P())
    out_specs = P(freq, None, None, chan, None)
    return jax.shard_map(local, mesh=fine, in_specs=in_specs, out_specs=out_specs, check_vma=False)
```

```python
import functools
import math

import jax
import jax.numpy as jnp
import numpy as np
from jax import lax
from jax.experimental import pallas as pl
from jax.experimental.pallas import tpu as pltpu
from jax.sharding import Mesh
from jax.sharding import PartitionSpec as P

CH = 128
NT = 512
BIN0 = 8
GROUP = 5
CHUNKS = (10, 10)
NOFF = 9


def grant(mib):
    return pltpu.CompilerParams(vmem_limit_bytes=mib * 1024 * 1024)


def basis_rows(groups):
    t = np.arange(NT)
    bins = BIN0 + np.arange(2 * groups)
    phase = (t[:, None] * bins[None, :] % NT).astype(np.float32)
    angles = np.float32(2.0 * math.pi / NT) * phase
    taper = np.float32(0.5) - np.float32(0.5) * np.cos(np.float32(2.0 * math.pi / NT) * t.astype(np.float32))
    table = np.stack([taper[:, None] * np.cos(angles), -taper[:, None] * np.sin(angles)], axis=2)
    table = table.reshape(NT, groups, 4).transpose(2, 1, 0).reshape(4 * groups, NT)
    return jnp.asarray(table.astype(jnp.bfloat16))


def spectra_body(*refs, first, count, groups):
    (strain, *small), out = refs[:5], refs[5]
    held, live, order, basis, whiten, place, packed, loaded, ready, gone = refs[6:]
    rows = 4 * count
    copies = []
    for i in range(count // GROUP):
        part = pl.ds(first + i * GROUP, GROUP)
        copies.append(pltpu.make_async_copy(strain.at[part], held.at[pl.ds(i * GROUP, GROUP)], loaded.at[i]))
    fixed = [
        pltpu.make_async_copy(source, target, ready.at[i])
        for i, (source, target) in enumerate(zip(small, (live, order, basis, whiten)))
    ]
    for copy in [*fixed, *copies]:
        copy.start()
    for copy in fixed:
        copy.wait()
    channel = lax.broadcasted_iota(jnp.int32, (CH, CH), 0)
    pick = (channel == order[...]).astype(jnp.float32).astype(jnp.bfloat16)
    shape = (4 * groups, 2 * groups)
    row = lax.broadcasted_iota(jnp.int32, shape, 0)
    column = lax.broadcasted_iota(jnp.int32, shape, 1)
    spread = jnp.where(column == 2 * (row % groups) + row // (2 * groups), whiten[...], 0.0)
    gain = jnp.sum(spread, axis=1, keepdims=True) * (2.0 / math.sqrt(NT))
    for i in range(count // GROUP):
        copies[i].wait()
        for at in range(i * GROUP, (i + 1) * GROUP):
            value = held[at].astype(jnp.float32)
            centered = value - jnp.sum(value, axis=1, keepdims=True) * (1.0 / NT)
            power = jnp.sum(centered * centered, axis=1, keepdims=True) * (1.0 / NT)
            normed = (centered * lax.rsqrt(power + 1e-06)).astype(jnp.bfloat16)
            spec = lax.dot_general(basis[...], normed, (((1,), (1,)), ((), ())), preferred_element_type=jnp.float32)
            weight = live[first + at : first + at + 1, :].astype(jnp.float32)
            spec = (spec * gain * weight).astype(jnp.bfloat16)
            spec = jnp.dot(spec, pick, preferred_element_type=jnp.float32)
            for part in range(4):
                place[pl.ds(at * 4 + part, groups, stride=rows), :] = spec[part * groups : (part + 1) * groups]
    copies = []
    for x in range(4):
        size = groups * rows // 4
        packed[x] = place[x * size : (x + 1) * size].astype(jnp.bfloat16)
        for half in range(2):
            copies.append(pltpu.make_async_copy(packed.at[x], out.at[x, half], gone.at[x, half]))
            copies[-1].start()
    for copy in copies:
        copy.wait()


def spectra(strain, live, order, basis, whiten, first, count):
    groups = basis.shape[0] // 4
    rows = 4 * count
    somewhere = pl.BlockSpec(memory_space=pl.ANY)
    small = (live, order, basis, whiten)
    return pl.pallas_call(
        functools.partial(spectra_body, first=first, count=count, groups=groups),
        in_specs=[somewhere] * 5,
        out_specs=somewhere,
        out_shape=jax.ShapeDtypeStruct((4, 2, groups * rows // 4, CH), jnp.bfloat16),
        scratch_shapes=[
            pltpu.VMEM((count, CH, NT), jnp.bfloat16),
            *[pltpu.VMEM(v.shape, v.dtype) for v in small],
            pltpu.VMEM((groups * rows, CH), jnp.float32),
            pltpu.VMEM((4, groups * rows // 4, CH), jnp.bfloat16),
            pltpu.SemaphoreType.DMA((count // GROUP,)),
            pltpu.SemaphoreType.DMA((4,)),
            pltpu.SemaphoreType.DMA((4, 2)),
        ],
        name="spectra",
    )(strain, *small)


def left_body(where, data, out):
    own = data[:, where[0]]
    own = own.reshape(-1, CH).astype(jnp.float32)
    own = own.reshape(-1, 8, CH)
    part = lax.broadcasted_iota(jnp.int32, own.shape, 1)
    turned = jnp.where(part % 2 == 0, pltpu.roll(own, 7, 1), -pltpu.roll(own, 1, 1))
    own = own.reshape(-1, CH).T
    turned = turned.reshape(-1, CH).T
    first = lax.broadcasted_iota(jnp.int32, own.shape, 1) % 4 < 2
    zero = jnp.zeros_like(own)
    out[0 * CH : 1 * CH] = jnp.where(first, own, zero).astype(jnp.bfloat16)
    out[1 * CH : 2 * CH] = jnp.where(first, turned, zero).astype(jnp.bfloat16)
    out[2 * CH : 3 * CH] = jnp.where(first, zero, own).astype(jnp.bfloat16)
    out[3 * CH : 4 * CH] = jnp.where(first, zero, turned).astype(jnp.bfloat16)


def left_of(where, data):
    whole = pl.BlockSpec(memory_space=pltpu.VMEM)
    return pl.pallas_call(
        left_body,
        in_specs=[pl.BlockSpec(memory_space=pltpu.SMEM), whole],
        out_specs=whole,
        out_shape=jax.ShapeDtypeStruct((4 * CH, data.shape[0] * data.shape[2]), jnp.bfloat16),
        compiler_params=grant(12),
        name="left",
    )(where, data)


def product(left, ref):
    right = jnp.concatenate([ref[:, 0].reshape(-1, CH), ref[:, 1].reshape(-1, CH)], axis=1)
    return jnp.dot(left[...], right, preferred_element_type=jnp.float32)


def early_body(left, *refs):
    for i in range(6):
        refs[6 + i // 2][i % 2] = product(left, refs[i])


def early(left, data):
    whole = pl.BlockSpec(memory_space=pltpu.VMEM)
    return pl.pallas_call(
        early_body,
        in_specs=[whole] * 7,
        out_specs=[whole] * 3,
        out_shape=[jax.ShapeDtypeStruct((2, 4 * CH, 2 * CH), jnp.float32)] * 3,
        cost_estimate=pl.CostEstimate(flops=20 * 10**9, transcendentals=0, bytes_accessed=12 * 10**6),
        compiler_params=grant(24),
        name="early",
    )(left, *data)


def late_body(where, left, begun, one, two, *refs, ahead, scale):
    out, stage, done = refs[-3:]
    half, core = where[0], where[1]
    jobs = []
    for other, ref in enumerate((one, two)):
        total = (begun[other] + product(left, ref)) * scale
        for side in range(2):
            spot = 2 * other + side
            for part in range(4):
                row = part * CH
                stage[spot, part // 2, part % 2] = total[row : row + CH, side * CH : (side + 1) * CH]
            offset = 4 * ahead + 2 * (side - half) + other * (1 - 2 * core)
            valid = jnp.logical_and(offset >= 0, offset < NOFF)
            target = jnp.clip(offset, 0, NOFF - 1)
            copy = pltpu.make_async_copy(stage.at[spot], out.at[:, :, target], done.at[spot])
            jobs.append((valid, copy))
            pl.when(valid)(copy.start)
    for valid, copy in jobs:
        pl.when(valid)(copy.wait)


def late(where, left, begun, one, two, filled, ahead, scale):
    whole = pl.BlockSpec(memory_space=pltpu.VMEM)
    somewhere = pl.BlockSpec(memory_space=pl.ANY)
    extra = [] if filled is None else [filled]
    return pl.pallas_call(
        functools.partial(late_body, ahead=ahead, scale=scale),
        in_specs=[
            pl.BlockSpec(memory_space=pltpu.SMEM),
            whole,
            whole,
            whole,
            whole,
        ]
        + [somewhere] * len(extra),
        out_specs=somewhere,
        out_shape=jax.ShapeDtypeStruct((2, 2, NOFF, CH, CH), jnp.float32),
        input_output_aliases={5: 0} if extra else {},
        scratch_shapes=[pltpu.VMEM((4, 2, 2, CH, CH), jnp.float32), pltpu.SemaphoreType.DMA((4,))],
        cost_estimate=pl.CostEstimate(flops=4 * 10**9, transcendentals=0, bytes_accessed=4 * 10**6),
        compiler_params=grant(16),
        name="late",
    )(where, left, begun, one, two, *extra)


def shifted(value, axis, steps):
    count = lax.axis_size(axis)
    return lax.ppermute(value, axis, [(s, (s + steps) % count) for s in range(count)])


def upper(value, steps):
    count = lax.axis_size("y")
    pairs = [(2 * y + 1, 2 * ((y + steps) % count) + 1) for y in range(count)]
    return lax.ppermute(value, ("y", "z_hi"), pairs)


def fetched(here, held):
    ahead1 = shifted(here, "y", -1)
    high = upper(here[:, 1], 2)
    low, here, *held = lax.optimization_barrier((shifted(here[:, 0], "y", 1), here, *held))
    return [here, ahead1, (shifted(low, "y", 1), high)], held


def both(own):
    return [w for v in own for w in (v, shifted(v, "core", 1))]


def local(strain, fiber_order, window_valid, whiten):
    groups = whiten.shape[0] // 2
    windows = strain.shape[1]
    strain = jnp.transpose(strain, (1, 0, 2))
    live = jnp.transpose(window_valid)
    basis = basis_rows(groups)
    where = jnp.stack([lax.axis_index("z_hi"), lax.axis_index("core")]).astype(jnp.int32)
    scale = 1.0 / math.sqrt(windows * lax.axis_size("x") * lax.axis_size("z_lo"))

    def made(first, count):
        sent = spectra(strain, live, fiber_order, basis, whiten.reshape(1, -1), first, count)
        return sent.reshape(2 * groups, 4 * count, CH)

    def spread(sent):
        here = lax.all_to_all(sent, ("x", "z_hi", "z_lo"), 0, 0, tiled=True)
        return here.reshape(4, 2, -1, CH)

    first, second = spread(made(0, CHUNKS[0])), made(*CHUNKS)
    first, second = lax.optimization_barrier((first, second))
    (first, ahead1, ahead2), _ = fetched(first, [])
    head = both([first, ahead1, jnp.stack(ahead2, axis=1)])
    tail = spread(second)
    tail, *head = lax.optimization_barrier((tail, *head))
    (tail, ahead1, ahead2), head = fetched(tail, head)
    begun = early(left_of(where, head[0]), head)
    left = left_of(where, tail)
    filled = late(where, left, begun[0], tail, shifted(tail, "core", 1), None, 0, scale)
    ahead1, ahead2, filled = lax.optimization_barrier((ahead1, ahead2, filled))
    other1 = shifted(ahead1, "core", 1)
    ahead2 = jnp.stack(ahead2, axis=1)
    other2 = shifted(ahead2, "core", 1)
    filled = late(where, left, begun[1], ahead1, other1, filled, 1, scale)
    return late(where, left, begun[2], ahead2, other2, filled, 2, scale)


def solution(mesh):
    fine = Mesh(mesh.devices.reshape(4, 8, 4, 2, 2), ("x", "z_lo", "y", "z_hi", "core"))
    freq, chan = ("x", "z_lo"), ("y", "z_hi", "core")
    in_specs = (P(chan, freq, None), P(chan, None), P(chan, freq), P())
    out_specs = P(freq, None, None, chan, None)
    return jax.shard_map(local, mesh=fine, in_specs=in_specs, out_specs=out_specs, check_vma=False)
```

```python
import functools
import math

import jax
import jax.numpy as jnp
import numpy as np
from jax import lax
from jax.experimental import pallas as pl
from jax.experimental.pallas import tpu as pltpu
from jax.sharding import Mesh
from jax.sharding import PartitionSpec as P

CH = 128
NT = 512
BIN0 = 8
GROUP = 4
CHUNKS = (12, 8)
NOFF = 9


def grant(mib):
    return pltpu.CompilerParams(vmem_limit_bytes=mib * 1024 * 1024)


def basis_rows(groups):
    t = np.arange(NT)
    bins = BIN0 + np.arange(2 * groups)
    phase = (t[:, None] * bins[None, :] % NT).astype(np.float32)
    angles = np.float32(2.0 * math.pi / NT) * phase
    taper = np.float32(0.5) - np.float32(0.5) * np.cos(np.float32(2.0 * math.pi / NT) * t.astype(np.float32))
    table = np.stack([taper[:, None] * np.cos(angles), -taper[:, None] * np.sin(angles)], axis=2)
    table = table.reshape(NT, groups, 4).transpose(2, 1, 0).reshape(4 * groups, NT)
    return jnp.asarray(table.astype(jnp.bfloat16))


def spectra_body(*refs, first, count, groups):
    (strain, *small), out = refs[:5], refs[5]
    held, live, order, basis, whiten, place, packed, loaded, ready, gone = refs[6:]
    rows = 4 * count
    copies = []
    for i in range(count // GROUP):
        part = pl.ds(first + i * GROUP, GROUP)
        copies.append(pltpu.make_async_copy(strain.at[part], held.at[pl.ds(i * GROUP, GROUP)], loaded.at[i]))
    fixed = [
        pltpu.make_async_copy(source, target, ready.at[i])
        for i, (source, target) in enumerate(zip(small, (live, order, basis, whiten)))
    ]
    for copy in [*fixed, *copies]:
        copy.start()
    for copy in fixed:
        copy.wait()
    channel = lax.broadcasted_iota(jnp.int32, (CH, CH), 0)
    pick = (channel == order[...]).astype(jnp.float32).astype(jnp.bfloat16)
    shape = (4 * groups, 2 * groups)
    row = lax.broadcasted_iota(jnp.int32, shape, 0)
    column = lax.broadcasted_iota(jnp.int32, shape, 1)
    spread = jnp.where(column == 2 * (row % groups) + row // (2 * groups), whiten[...], 0.0)
    gain = jnp.sum(spread, axis=1, keepdims=True) * (2.0 / math.sqrt(NT))
    for i in range(count // GROUP):
        copies[i].wait()
        for at in range(i * GROUP, (i + 1) * GROUP):
            value = held[at].astype(jnp.float32)
            centered = value - jnp.sum(value, axis=1, keepdims=True) * (1.0 / NT)
            power = jnp.sum(centered * centered, axis=1, keepdims=True) * (1.0 / NT)
            normed = (centered * lax.rsqrt(power + 1e-06)).astype(jnp.bfloat16)
            spec = lax.dot_general(basis[...], normed, (((1,), (1,)), ((), ())), preferred_element_type=jnp.float32)
            weight = live[first + at : first + at + 1, :].astype(jnp.float32)
            spec = (spec * gain * weight).astype(jnp.bfloat16)
            spec = jnp.dot(spec, pick, preferred_element_type=jnp.float32)
            for part in range(4):
                place[pl.ds(at * 4 + part, groups, stride=rows), :] = spec[part * groups : (part + 1) * groups]
    copies = []
    for x in range(4):
        size = groups * rows // 4
        packed[x] = place[x * size : (x + 1) * size].astype(jnp.bfloat16)
        for half in range(2):
            copies.append(pltpu.make_async_copy(packed.at[x], out.at[x, half], gone.at[x, half]))
            copies[-1].start()
    for copy in copies:
        copy.wait()


def spectra(strain, live, order, basis, whiten, first, count):
    groups = basis.shape[0] // 4
    rows = 4 * count
    somewhere = pl.BlockSpec(memory_space=pl.ANY)
    small = (live, order, basis, whiten)
    return pl.pallas_call(
        functools.partial(spectra_body, first=first, count=count, groups=groups),
        in_specs=[somewhere] * 5,
        out_specs=somewhere,
        out_shape=jax.ShapeDtypeStruct((4, 2, groups * rows // 4, CH), jnp.bfloat16),
        scratch_shapes=[
            pltpu.VMEM((count, CH, NT), jnp.bfloat16),
            *[pltpu.VMEM(v.shape, v.dtype) for v in small],
            pltpu.VMEM((groups * rows, CH), jnp.float32),
            pltpu.VMEM((4, groups * rows // 4, CH), jnp.bfloat16),
            pltpu.SemaphoreType.DMA((count // GROUP,)),
            pltpu.SemaphoreType.DMA((4,)),
            pltpu.SemaphoreType.DMA((4, 2)),
        ],
        name="spectra",
    )(strain, *small)


def left_body(where, data, out):
    own = data[:, where[0]]
    own = own.reshape(-1, CH).astype(jnp.float32)
    own = own.reshape(-1, 8, CH)
    part = lax.broadcasted_iota(jnp.int32, own.shape, 1)
    turned = jnp.where(part % 2 == 0, pltpu.roll(own, 7, 1), -pltpu.roll(own, 1, 1))
    own = own.reshape(-1, CH).T
    turned = turned.reshape(-1, CH).T
    first = lax.broadcasted_iota(jnp.int32, own.shape, 1) % 4 < 2
    zero = jnp.zeros_like(own)
    out[0 * CH : 1 * CH] = jnp.where(first, own, zero).astype(jnp.bfloat16)
    out[1 * CH : 2 * CH] = jnp.where(first, turned, zero).astype(jnp.bfloat16)
    out[2 * CH : 3 * CH] = jnp.where(first, zero, own).astype(jnp.bfloat16)
    out[3 * CH : 4 * CH] = jnp.where(first, zero, turned).astype(jnp.bfloat16)


def left_of(where, data):
    whole = pl.BlockSpec(memory_space=pltpu.VMEM)
    return pl.pallas_call(
        left_body,
        in_specs=[pl.BlockSpec(memory_space=pltpu.SMEM), whole],
        out_specs=whole,
        out_shape=jax.ShapeDtypeStruct((4 * CH, data.shape[0] * data.shape[2]), jnp.bfloat16),
        compiler_params=grant(12),
        name="left",
    )(where, data)


def product(left, ref):
    right = jnp.concatenate([ref[:, 0].reshape(-1, CH), ref[:, 1].reshape(-1, CH)], axis=1)
    return jnp.dot(left[...], right, preferred_element_type=jnp.float32)


def early_body(left, *refs):
    for i in range(6):
        refs[6 + i // 2][i % 2] = product(left, refs[i])


def early(left, data):
    whole = pl.BlockSpec(memory_space=pltpu.VMEM)
    return pl.pallas_call(
        early_body,
        in_specs=[whole] * 7,
        out_specs=[whole] * 3,
        out_shape=[jax.ShapeDtypeStruct((2, 4 * CH, 2 * CH), jnp.float32)] * 3,
        cost_estimate=pl.CostEstimate(flops=20 * 10**9, transcendentals=0, bytes_accessed=12 * 10**6),
        compiler_params=grant(24),
        name="early",
    )(left, *data)


def late_body(where, left, begun, one, two, *refs, ahead, scale):
    out, stage, done = refs[-3:]
    half, core = where[0], where[1]
    jobs = []
    for other, ref in enumerate((one, two)):
        total = (begun[other] + product(left, ref)) * scale
        for side in range(2):
            spot = 2 * other + side
            for part in range(4):
                row = part * CH
                stage[spot, part // 2, part % 2] = total[row : row + CH, side * CH : (side + 1) * CH]
            offset = 4 * ahead + 2 * (side - half) + other * (1 - 2 * core)
            valid = jnp.logical_and(offset >= 0, offset < NOFF)
            target = jnp.clip(offset, 0, NOFF - 1)
            copy = pltpu.make_async_copy(stage.at[spot], out.at[:, :, target], done.at[spot])
            jobs.append((valid, copy))
            pl.when(valid)(copy.start)
    for valid, copy in jobs:
        pl.when(valid)(copy.wait)


def late(where, left, begun, one, two, filled, ahead, scale):
    whole = pl.BlockSpec(memory_space=pltpu.VMEM)
    somewhere = pl.BlockSpec(memory_space=pl.ANY)
    extra = [] if filled is None else [filled]
    return pl.pallas_call(
        functools.partial(late_body, ahead=ahead, scale=scale),
        in_specs=[
            pl.BlockSpec(memory_space=pltpu.SMEM),
            whole,
            whole,
            whole,
            whole,
        ]
        + [somewhere] * len(extra),
        out_specs=somewhere,
        out_shape=jax.ShapeDtypeStruct((2, 2, NOFF, CH, CH), jnp.float32),
        input_output_aliases={5: 0} if extra else {},
        scratch_shapes=[pltpu.VMEM((4, 2, 2, CH, CH), jnp.float32), pltpu.SemaphoreType.DMA((4,))],
        cost_estimate=pl.CostEstimate(flops=4 * 10**9, transcendentals=0, bytes_accessed=4 * 10**6),
        compiler_params=grant(16),
        name="late",
    )(where, left, begun, one, two, *extra)


def shifted(value, axis, steps):
    count = lax.axis_size(axis)
    return lax.ppermute(value, axis, [(s, (s + steps) % count) for s in range(count)])


def upper(value, steps):
    count = lax.axis_size("y")
    pairs = [(2 * y + 1, 2 * ((y + steps) % count) + 1) for y in range(count)]
    return lax.ppermute(value, ("y", "z_hi"), pairs)


def fetched(here, held):
    ahead1 = shifted(here, "y", -1)
    high = upper(here[:, 1], 2)
    low, here, *held = lax.optimization_barrier((shifted(here[:, 0], "y", 1), here, *held))
    return [here, ahead1, (shifted(low, "y", 1), high)], held


def both(own):
    return [w for v in own for w in (v, shifted(v, "core", 1))]


def local(strain, fiber_order, window_valid, whiten):
    groups = whiten.shape[0] // 2
    windows = strain.shape[1]
    strain = jnp.transpose(strain, (1, 0, 2))
    live = jnp.transpose(window_valid)
    basis = basis_rows(groups)
    where = jnp.stack([lax.axis_index("z_hi"), lax.axis_index("core")]).astype(jnp.int32)
    scale = 1.0 / math.sqrt(windows * lax.axis_size("x") * lax.axis_size("z_lo"))

    def made(first, count):
        sent = spectra(strain, live, fiber_order, basis, whiten.reshape(1, -1), first, count)
        return sent.reshape(2 * groups, 4 * count, CH)

    def spread(sent):
        here = lax.all_to_all(sent, ("x", "z_hi", "z_lo"), 0, 0, tiled=True)
        return here.reshape(4, 2, -1, CH)

    first, second = spread(made(0, CHUNKS[0])), made(*CHUNKS)
    first, second = lax.optimization_barrier((first, second))
    (first, ahead1, ahead2), _ = fetched(first, [])
    head = both([first, ahead1, jnp.stack(ahead2, axis=1)])
    tail = spread(second)
    tail, *head = lax.optimization_barrier((tail, *head))
    (tail, ahead1, ahead2), head = fetched(tail, head)
    begun = early(left_of(where, head[0]), head)
    left = left_of(where, tail)
    filled = late(where, left, begun[0], tail, shifted(tail, "core", 1), None, 0, scale)
    ahead1, ahead2, filled = lax.optimization_barrier((ahead1, ahead2, filled))
    other1 = shifted(ahead1, "core", 1)
    ahead2 = jnp.stack(ahead2, axis=1)
    other2 = shifted(ahead2, "core", 1)
    filled = late(where, left, begun[1], ahead1, other1, filled, 1, scale)
    return late(where, left, begun[2], ahead2, other2, filled, 2, scale)


def solution(mesh):
    fine = Mesh(mesh.devices.reshape(4, 8, 4, 2, 2), ("x", "z_lo", "y", "z_hi", "core"))
    freq, chan = ("x", "z_lo"), ("y", "z_hi", "core")
    in_specs = (P(chan, freq, None), P(chan, None), P(chan, freq), P())
    out_specs = P(freq, None, None, chan, None)
    return jax.shard_map(local, mesh=fine, in_specs=in_specs, out_specs=out_specs, check_vma=False)
```

```python
import functools
import math

import jax
import jax.numpy as jnp
import numpy as np
from jax import lax
from jax.experimental import pallas as pl
from jax.experimental.pallas import tpu as pltpu
from jax.sharding import Mesh
from jax.sharding import PartitionSpec as P

CH = 128
NT = 512
BIN0 = 8
GROUP = 5
CHUNKS = (10, 10)
NOFF = 9


def grant(mib):
    return pltpu.CompilerParams(vmem_limit_bytes=mib * 1024 * 1024)


def basis_rows(groups):
    t = np.arange(NT)
    bins = BIN0 + np.arange(2 * groups)
    phase = (t[:, None] * bins[None, :] % NT).astype(np.float32)
    angles = np.float32(2.0 * math.pi / NT) * phase
    taper = np.float32(0.5) - np.float32(0.5) * np.cos(np.float32(2.0 * math.pi / NT) * t.astype(np.float32))
    table = np.stack([taper[:, None] * np.cos(angles), -taper[:, None] * np.sin(angles)], axis=2)
    table = table.reshape(NT, groups, 4).transpose(2, 1, 0).reshape(4 * groups, NT)
    return jnp.asarray(table.astype(jnp.bfloat16))


def spectra_body(*refs, first, count, groups):
    (strain, *small), out = refs[:5], refs[5]
    held, live, order, basis, whiten, place, packed, loaded, ready, gone = refs[6:]
    rows = 4 * count
    copies = []
    for i in range(count // GROUP):
        part = pl.ds(first + i * GROUP, GROUP)
        copies.append(pltpu.make_async_copy(strain.at[part], held.at[pl.ds(i * GROUP, GROUP)], loaded.at[i]))
    fixed = [
        pltpu.make_async_copy(source, target, ready.at[i])
        for i, (source, target) in enumerate(zip(small, (live, order, basis, whiten)))
    ]
    for copy in [*fixed, *copies]:
        copy.start()
    for copy in fixed:
        copy.wait()
    channel = lax.broadcasted_iota(jnp.int32, (CH, CH), 0)
    pick = (channel == order[...]).astype(jnp.float32).astype(jnp.bfloat16)
    shape = (4 * groups, 2 * groups)
    row = lax.broadcasted_iota(jnp.int32, shape, 0)
    column = lax.broadcasted_iota(jnp.int32, shape, 1)
    spread = jnp.where(column == 2 * (row % groups) + row // (2 * groups), whiten[...], 0.0)
    gain = jnp.sum(spread, axis=1, keepdims=True) * (2.0 / math.sqrt(NT))
    for i in range(count // GROUP):
        copies[i].wait()
        for at in range(i * GROUP, (i + 1) * GROUP):
            value = held[at].astype(jnp.float32)
            centered = value - jnp.sum(value, axis=1, keepdims=True) * (1.0 / NT)
            power = jnp.sum(centered * centered, axis=1, keepdims=True) * (1.0 / NT)
            normed = (centered * lax.rsqrt(power + 1e-06)).astype(jnp.bfloat16)
            spec = lax.dot_general(basis[...], normed, (((1,), (1,)), ((), ())), preferred_element_type=jnp.float32)
            weight = live[first + at : first + at + 1, :].astype(jnp.float32)
            spec = (spec * gain * weight).astype(jnp.bfloat16)
            spec = jnp.dot(spec, pick, preferred_element_type=jnp.float32)
            for part in range(4):
                place[pl.ds(at * 4 + part, groups, stride=rows), :] = spec[part * groups : (part + 1) * groups]
    copies = []
    for x in range(4):
        size = groups * rows // 4
        packed[x] = place[x * size : (x + 1) * size].astype(jnp.bfloat16)
        for half in range(2):
            copies.append(pltpu.make_async_copy(packed.at[x], out.at[x, half], gone.at[x, half]))
            copies[-1].start()
    for copy in copies:
        copy.wait()


def spectra(strain, live, order, basis, whiten, first, count):
    groups = basis.shape[0] // 4
    rows = 4 * count
    somewhere = pl.BlockSpec(memory_space=pl.ANY)
    small = (live, order, basis, whiten)
    return pl.pallas_call(
        functools.partial(spectra_body, first=first, count=count, groups=groups),
        in_specs=[somewhere] * 5,
        out_specs=somewhere,
        out_shape=jax.ShapeDtypeStruct((4, 2, groups * rows // 4, CH), jnp.bfloat16),
        scratch_shapes=[
            pltpu.VMEM((count, CH, NT), jnp.bfloat16),
            *[pltpu.VMEM(v.shape, v.dtype) for v in small],
            pltpu.VMEM((groups * rows, CH), jnp.float32),
            pltpu.VMEM((4, groups * rows // 4, CH), jnp.bfloat16),
            pltpu.SemaphoreType.DMA((count // GROUP,)),
            pltpu.SemaphoreType.DMA((4,)),
            pltpu.SemaphoreType.DMA((4, 2)),
        ],
        name="spectra",
    )(strain, *small)


def left_body(where, data, out):
    own = data[:, where[0]]
    own = own.reshape(-1, CH).astype(jnp.float32)
    own = own.reshape(-1, 8, CH)
    part = lax.broadcasted_iota(jnp.int32, own.shape, 1)
    turned = jnp.where(part % 2 == 0, pltpu.roll(own, 7, 1), -pltpu.roll(own, 1, 1))
    own = own.reshape(-1, CH).T
    turned = turned.reshape(-1, CH).T
    first = lax.broadcasted_iota(jnp.int32, own.shape, 1) % 4 < 2
    zero = jnp.zeros_like(own)
    out[0 * CH : 1 * CH] = jnp.where(first, own, zero).astype(jnp.bfloat16)
    out[1 * CH : 2 * CH] = jnp.where(first, turned, zero).astype(jnp.bfloat16)
    out[2 * CH : 3 * CH] = jnp.where(first, zero, own).astype(jnp.bfloat16)
    out[3 * CH : 4 * CH] = jnp.where(first, zero, turned).astype(jnp.bfloat16)


def left_of(where, data):
    whole = pl.BlockSpec(memory_space=pltpu.VMEM)
    return pl.pallas_call(
        left_body,
        in_specs=[pl.BlockSpec(memory_space=pltpu.SMEM), whole],
        out_specs=whole,
        out_shape=jax.ShapeDtypeStruct((4 * CH, data.shape[0] * data.shape[2]), jnp.bfloat16),
        compiler_params=grant(12),
        name="left",
    )(where, data)


def product(left, ref):
    right = jnp.concatenate([ref[:, 0].reshape(-1, CH), ref[:, 1].reshape(-1, CH)], axis=1)
    return jnp.dot(left[...], right, preferred_element_type=jnp.float32)


def early_body(left, *refs):
    for i in range(6):
        refs[6 + i // 2][i % 2] = product(left, refs[i])


def early(left, data):
    whole = pl.BlockSpec(memory_space=pltpu.VMEM)
    return pl.pallas_call(
        early_body,
        in_specs=[whole] * 7,
        out_specs=[whole] * 3,
        out_shape=[jax.ShapeDtypeStruct((2, 4 * CH, 2 * CH), jnp.float32)] * 3,
        cost_estimate=pl.CostEstimate(flops=1 * 10**8, transcendentals=0, bytes_accessed=10**5),
        compiler_params=grant(24),
        name="early",
    )(left, *data)


def late_body(where, left, begun, one, two, *refs, ahead, scale):
    out, stage, done = refs[-3:]
    half, core = where[0], where[1]
    jobs = []
    for other, ref in enumerate((one, two)):
        total = (begun[other] + product(left, ref)) * scale
        for side in range(2):
            spot = 2 * other + side
            for part in range(4):
                row = part * CH
                stage[spot, part // 2, part % 2] = total[row : row + CH, side * CH : (side + 1) * CH]
            offset = 4 * ahead + 2 * (side - half) + other * (1 - 2 * core)
            valid = jnp.logical_and(offset >= 0, offset < NOFF)
            target = jnp.clip(offset, 0, NOFF - 1)
            copy = pltpu.make_async_copy(stage.at[spot], out.at[:, :, target], done.at[spot])
            jobs.append((valid, copy))
            pl.when(valid)(copy.start)
    for valid, copy in jobs:
        pl.when(valid)(copy.wait)


def late(where, left, begun, one, two, filled, ahead, scale):
    whole = pl.BlockSpec(memory_space=pltpu.VMEM)
    somewhere = pl.BlockSpec(memory_space=pl.ANY)
    extra = [] if filled is None else [filled]
    return pl.pallas_call(
        functools.partial(late_body, ahead=ahead, scale=scale),
        in_specs=[
            pl.BlockSpec(memory_space=pltpu.SMEM),
            whole,
            whole,
            whole,
            whole,
        ]
        + [somewhere] * len(extra),
        out_specs=somewhere,
        out_shape=jax.ShapeDtypeStruct((2, 2, NOFF, CH, CH), jnp.float32),
        input_output_aliases={5: 0} if extra else {},
        scratch_shapes=[pltpu.VMEM((4, 2, 2, CH, CH), jnp.float32), pltpu.SemaphoreType.DMA((4,))],
        cost_estimate=pl.CostEstimate(flops=1 * 10**8, transcendentals=0, bytes_accessed=10**5),
        compiler_params=grant(16),
        name="late",
    )(where, left, begun, one, two, *extra)


def shifted(value, axis, steps):
    count = lax.axis_size(axis)
    return lax.ppermute(value, axis, [(s, (s + steps) % count) for s in range(count)])


def upper(value, steps):
    count = lax.axis_size("y")
    pairs = [(2 * y + 1, 2 * ((y + steps) % count) + 1) for y in range(count)]
    return lax.ppermute(value, ("y", "z_hi"), pairs)


def fetched(here, held):
    ahead1 = shifted(here, "y", -1)
    high = upper(here[:, 1], 2)
    low, here, *held = lax.optimization_barrier((shifted(here[:, 0], "y", 1), here, *held))
    return [here, ahead1, (shifted(low, "y", 1), high)], held


def both(own):
    return [w for v in own for w in (v, shifted(v, "core", 1))]


def local(strain, fiber_order, window_valid, whiten):
    groups = whiten.shape[0] // 2
    windows = strain.shape[1]
    strain = jnp.transpose(strain, (1, 0, 2))
    live = jnp.transpose(window_valid)
    basis = basis_rows(groups)
    where = jnp.stack([lax.axis_index("z_hi"), lax.axis_index("core")]).astype(jnp.int32)
    scale = 1.0 / math.sqrt(windows * lax.axis_size("x") * lax.axis_size("z_lo"))

    def made(first, count):
        sent = spectra(strain, live, fiber_order, basis, whiten.reshape(1, -1), first, count)
        return sent.reshape(2 * groups, 4 * count, CH)

    def spread(sent):
        here = lax.all_to_all(sent, ("x", "z_hi", "z_lo"), 0, 0, tiled=True)
        return here.reshape(4, 2, -1, CH)

    first, second = spread(made(0, CHUNKS[0])), made(*CHUNKS)
    first, second = lax.optimization_barrier((first, second))
    (first, ahead1, ahead2), _ = fetched(first, [])
    head = both([first, ahead1, jnp.stack(ahead2, axis=1)])
    tail = spread(second)
    tail, *head = lax.optimization_barrier((tail, *head))
    (own, ahead1, ahead2), _ = fetched(tail, [])
    begun = early(left_of(where, head[0]), head)
    left = left_of(where, tail)
    filled = late(where, left, begun[0], tail, shifted(tail, "core", 1), None, 0, scale)
    ahead1, ahead2, filled = lax.optimization_barrier((ahead1, ahead2, filled))
    other1 = shifted(ahead1, "core", 1)
    ahead2 = jnp.stack(ahead2, axis=1)
    other2 = shifted(ahead2, "core", 1)
    filled = late(where, left, begun[1], ahead1, other1, filled, 1, scale)
    return late(where, left, begun[2], ahead2, other2, filled, 2, scale)


def solution(mesh):
    fine = Mesh(mesh.devices.reshape(4, 8, 4, 2, 2), ("x", "z_lo", "y", "z_hi", "core"))
    freq, chan = ("x", "z_lo"), ("y", "z_hi", "core")
    in_specs = (P(chan, freq, None), P(chan, None), P(chan, freq), P())
    out_specs = P(freq, None, None, chan, None)
    return jax.shard_map(local, mesh=fine, in_specs=in_specs, out_specs=out_specs, check_vma=False)
```

```python
import functools
import math

import jax
import jax.numpy as jnp
import numpy as np
from jax import lax
from jax.experimental import pallas as pl
from jax.experimental.pallas import tpu as pltpu
from jax.sharding import Mesh
from jax.sharding import PartitionSpec as P

CH = 128
NT = 512
BIN0 = 8
GROUP = 5
CHUNKS = (10, 10)
NOFF = 9


def grant(mib):
    return pltpu.CompilerParams(vmem_limit_bytes=mib * 1024 * 1024)


def basis_rows(groups):
    t = np.arange(NT)
    bins = BIN0 + np.arange(2 * groups)
    phase = (t[:, None] * bins[None, :] % NT).astype(np.float32)
    angles = np.float32(2.0 * math.pi / NT) * phase
    taper = np.float32(0.5) - np.float32(0.5) * np.cos(np.float32(2.0 * math.pi / NT) * t.astype(np.float32))
    table = np.stack([taper[:, None] * np.cos(angles), -taper[:, None] * np.sin(angles)], axis=2)
    table = table.reshape(NT, groups, 4).transpose(2, 1, 0).reshape(4 * groups, NT)
    return jnp.asarray(table.astype(jnp.bfloat16))


def spectra_body(*refs, first, count, groups):
    (strain, *small), out = refs[:5], refs[5]
    held, live, order, basis, whiten, place, packed, loaded, ready, gone = refs[6:]
    rows = 4 * count
    copies = []
    for i in range(count // GROUP):
        part = pl.ds(first + i * GROUP, GROUP)
        copies.append(pltpu.make_async_copy(strain.at[part], held.at[pl.ds(i * GROUP, GROUP)], loaded.at[i]))
    fixed = [
        pltpu.make_async_copy(source, target, ready.at[i])
        for i, (source, target) in enumerate(zip(small, (live, order, basis, whiten)))
    ]
    for copy in [*fixed, *copies]:
        copy.start()
    for copy in fixed:
        copy.wait()
    channel = lax.broadcasted_iota(jnp.int32, (CH, CH), 0)
    pick = (channel == order[...]).astype(jnp.float32).astype(jnp.bfloat16)
    shape = (4 * groups, 2 * groups)
    row = lax.broadcasted_iota(jnp.int32, shape, 0)
    column = lax.broadcasted_iota(jnp.int32, shape, 1)
    spread = jnp.where(column == 2 * (row % groups) + row // (2 * groups), whiten[...], 0.0)
    gain = jnp.sum(spread, axis=1, keepdims=True) * (2.0 / math.sqrt(NT))
    for i in range(count // GROUP):
        copies[i].wait()
        for at in range(i * GROUP, (i + 1) * GROUP):
            value = held[at].astype(jnp.float32)
            centered = value - jnp.sum(value, axis=1, keepdims=True) * (1.0 / NT)
            power = jnp.sum(centered * centered, axis=1, keepdims=True) * (1.0 / NT)
            normed = (centered * lax.rsqrt(power + 1e-06)).astype(jnp.bfloat16)
            spec = lax.dot_general(basis[...], normed, (((1,), (1,)), ((), ())), preferred_element_type=jnp.float32)
            weight = live[first + at : first + at + 1, :].astype(jnp.float32)
            spec = (spec * gain * weight).astype(jnp.bfloat16)
            spec = jnp.dot(spec, pick, preferred_element_type=jnp.float32)
            for part in range(4):
                place[pl.ds(at * 4 + part, groups, stride=rows), :] = spec[part * groups : (part + 1) * groups]
    copies = []
    for x in range(4):
        size = groups * rows // 4
        packed[x] = place[x * size : (x + 1) * size].astype(jnp.bfloat16)
        for half in range(2):
            copies.append(pltpu.make_async_copy(packed.at[x], out.at[x, half], gone.at[x, half]))
            copies[-1].start()
    for copy in copies:
        copy.wait()


def spectra(strain, live, order, basis, whiten, first, count):
    groups = basis.shape[0] // 4
    rows = 4 * count
    somewhere = pl.BlockSpec(memory_space=pl.ANY)
    small = (live, order, basis, whiten)
    return pl.pallas_call(
        functools.partial(spectra_body, first=first, count=count, groups=groups),
        in_specs=[somewhere] * 5,
        out_specs=somewhere,
        out_shape=jax.ShapeDtypeStruct((4, 2, groups * rows // 4, CH), jnp.bfloat16),
        scratch_shapes=[
            pltpu.VMEM((count, CH, NT), jnp.bfloat16),
            *[pltpu.VMEM(v.shape, v.dtype) for v in small],
            pltpu.VMEM((groups * rows, CH), jnp.float32),
            pltpu.VMEM((4, groups * rows // 4, CH), jnp.bfloat16),
            pltpu.SemaphoreType.DMA((count // GROUP,)),
            pltpu.SemaphoreType.DMA((4,)),
            pltpu.SemaphoreType.DMA((4, 2)),
        ],
        name="spectra",
    )(strain, *small)


def left_body(where, data, out):
    own = data[:, where[0]]
    own = own.reshape(-1, CH).astype(jnp.float32)
    own = own.reshape(-1, 8, CH)
    part = lax.broadcasted_iota(jnp.int32, own.shape, 1)
    turned = jnp.where(part % 2 == 0, pltpu.roll(own, 7, 1), -pltpu.roll(own, 1, 1))
    own = own.reshape(-1, CH).T
    turned = turned.reshape(-1, CH).T
    first = lax.broadcasted_iota(jnp.int32, own.shape, 1) % 4 < 2
    zero = jnp.zeros_like(own)
    out[0 * CH : 1 * CH] = jnp.where(first, own, zero).astype(jnp.bfloat16)
    out[1 * CH : 2 * CH] = jnp.where(first, turned, zero).astype(jnp.bfloat16)
    out[2 * CH : 3 * CH] = jnp.where(first, zero, own).astype(jnp.bfloat16)
    out[3 * CH : 4 * CH] = jnp.where(first, zero, turned).astype(jnp.bfloat16)


def left_of(where, data):
    whole = pl.BlockSpec(memory_space=pltpu.VMEM)
    return pl.pallas_call(
        left_body,
        in_specs=[pl.BlockSpec(memory_space=pltpu.SMEM), whole],
        out_specs=whole,
        out_shape=jax.ShapeDtypeStruct((4 * CH, data.shape[0] * data.shape[2]), jnp.bfloat16),
        compiler_params=grant(12),
        name="left",
    )(where, data)


def product(left, ref):
    right = jnp.concatenate([ref[:, 0].reshape(-1, CH), ref[:, 1].reshape(-1, CH)], axis=1)
    return jnp.dot(left[...], right, preferred_element_type=jnp.float32)


def early_body(left, *refs):
    for i in range(6):
        refs[6 + i // 2][i % 2] = product(left, refs[i])


def early(left, data):
    whole = pl.BlockSpec(memory_space=pltpu.VMEM)
    return pl.pallas_call(
        early_body,
        in_specs=[whole] * 7,
        out_specs=[whole] * 3,
        out_shape=[jax.ShapeDtypeStruct((2, 4 * CH, 2 * CH), jnp.float32)] * 3,
        cost_estimate=pl.CostEstimate(flops=7 * 10**9, transcendentals=0, bytes_accessed=12 * 10**6),
        compiler_params=grant(24),
        name="early",
    )(left, *data)


def late_body(where, left, begun, one, two, *refs, ahead, scale):
    out, stage, done = refs[-3:]
    half, core = where[0], where[1]
    jobs = []
    for other, ref in enumerate((one, two)):
        total = (begun[other] + product(left, ref)) * scale
        for side in range(2):
            spot = 2 * other + side
            for part in range(4):
                row = part * CH
                stage[spot, part // 2, part % 2] = total[row : row + CH, side * CH : (side + 1) * CH]
            offset = 4 * ahead + 2 * (side - half) + other * (1 - 2 * core)
            valid = jnp.logical_and(offset >= 0, offset < NOFF)
            target = jnp.clip(offset, 0, NOFF - 1)
            copy = pltpu.make_async_copy(stage.at[spot], out.at[:, :, target], done.at[spot])
            jobs.append((valid, copy))
            pl.when(valid)(copy.start)
    for valid, copy in jobs:
        pl.when(valid)(copy.wait)


def late(where, left, begun, one, two, filled, ahead, scale):
    whole = pl.BlockSpec(memory_space=pltpu.VMEM)
    somewhere = pl.BlockSpec(memory_space=pl.ANY)
    extra = [] if filled is None else [filled]
    return pl.pallas_call(
        functools.partial(late_body, ahead=ahead, scale=scale),
        in_specs=[
            pl.BlockSpec(memory_space=pltpu.SMEM),
            whole,
            whole,
            whole,
            whole,
        ]
        + [somewhere] * len(extra),
        out_specs=somewhere,
        out_shape=jax.ShapeDtypeStruct((2, 2, NOFF, CH, CH), jnp.float32),
        input_output_aliases={5: 0} if extra else {},
        scratch_shapes=[pltpu.VMEM((4, 2, 2, CH, CH), jnp.float32), pltpu.SemaphoreType.DMA((4,))],
        cost_estimate=pl.CostEstimate(flops=2 * 10**9, transcendentals=0, bytes_accessed=4 * 10**6),
        compiler_params=grant(16),
        name="late",
    )(where, left, begun, one, two, *extra)


def shifted(value, axis, steps):
    count = lax.axis_size(axis)
    return lax.ppermute(value, axis, [(s, (s + steps) % count) for s in range(count)])


def upper(value, steps):
    count = lax.axis_size("y")
    pairs = [(2 * y + 1, 2 * ((y + steps) % count) + 1) for y in range(count)]
    return lax.ppermute(value, ("y", "z_hi"), pairs)


def fetched(here, held):
    ahead1 = shifted(here, "y", -1)
    low, *held = lax.optimization_barrier((shifted(here[:, 0], "y", 1), *held))
    return [here, ahead1, jnp.stack([shifted(low, "y", 1), upper(here[:, 1], 2)], axis=1)], held


def both(own):
    return [w for v in own for w in (v, shifted(v, "core", 1))]


def local(strain, fiber_order, window_valid, whiten):
    groups = whiten.shape[0] // 2
    windows = strain.shape[1]
    strain = jnp.transpose(strain, (1, 0, 2))
    live = jnp.transpose(window_valid)
    basis = basis_rows(groups)
    where = jnp.stack([lax.axis_index("z_hi"), lax.axis_index("core")]).astype(jnp.int32)
    scale = 1.0 / math.sqrt(windows * lax.axis_size("x") * lax.axis_size("z_lo"))

    def made(first, count):
        sent = spectra(strain, live, fiber_order, basis, whiten.reshape(1, -1), first, count)
        return sent.reshape(2 * groups, 4 * count, CH)

    def spread(sent):
        here = lax.all_to_all(sent, ("x", "z_hi", "z_lo"), 0, 0, tiled=True)
        return here.reshape(4, 2, -1, CH)

    first, second = spread(made(0, CHUNKS[0])), made(*CHUNKS)
    first, second = lax.optimization_barrier((first, second))
    head = both(fetched(first, [])[0])
    tail = spread(second)
    tail, *head = lax.optimization_barrier((tail, *head))
    (_, ahead1, ahead2), head = fetched(tail, head)
    begun = early(left_of(where, head[0]), head)
    left = left_of(where, tail)
    filled = late(where, left, begun[0], tail, shifted(tail, "core", 1), None, 0, scale)
    ahead1, ahead2, left, filled, *begun = lax.optimization_barrier((ahead1, ahead2, left, filled, *begun))
    data = both([ahead1, ahead2])
    for ahead in (1, 2):
        one, two = data[2 * ahead - 2 : 2 * ahead]
        filled = late(where, left, begun[ahead], one, two, filled, ahead, scale)
    return filled


def solution(mesh):
    fine = Mesh(mesh.devices.reshape(4, 8, 4, 2, 2), ("x", "z_lo", "y", "z_hi", "core"))
    freq, chan = ("x", "z_lo"), ("y", "z_hi", "core")
    in_specs = (P(chan, freq, None), P(chan, None), P(chan, freq), P())
    out_specs = P(freq, None, None, chan, None)
    return jax.shard_map(local, mesh=fine, in_specs=in_specs, out_specs=out_specs, check_vma=False)
```
